256 devices in a mesh: gx: 64 (over y, x, z_hi, core), gy: 4 (over z_lo).
Axes of the slice: x: 4, y: 4, z: 8 (z_hi: 2, z_lo: 4; z = z_hi * 4 + z_lo), core: 2. Of those that a mesh axis runs over, the one named last changes fastest.
Arguments:
- image: bfloat16 [32, 256, 16, 1024], P(None, 'gx', None, 'gy'), may hold values from -6 to 6
- w_first: bfloat16 [32, 32, 3, 3, 3], replicated, may hold values from -0.21875 to 0.21875
- b_first: float32 [32], replicated, may hold values from -3 to 3
- w_second: bfloat16 [64, 32, 3, 3, 3], replicated, may hold values from -0.21875 to 0.21875
- b_second: float32 [64], replicated, may hold values from -3 to 3
- w_third: bfloat16 [64, 64, 3, 3, 3], replicated, may hold values from -0.15625 to 0.15625
- b_third: float32 [64], replicated, may hold values from -3 to 3
Outputs:
- coarse_out: bfloat16 [64, 128, 8, 512], P(None, 'gx', None, 'gy')
The draws below stay inside these ranges and needn't reach their ends.
All inputs are finite; a program needn't handle non-finite values.
Results may differ from the reference program's by a relative error of at most 0.0056.
Values may be sent and summed in bfloat16 or wider, within the bound.
A program may use at most 64 MiB of HBM per device.

```python
import jax
import jax.numpy as jnp
from jax import lax

C1 = 32
C2 = 64
DEPTH = 16
NXH = 256
NYH = 1024


def levels(own_key, extent, split, least, high):
    gain = 1.0
    for dim, blocks in split:
        draws = jax.random.uniform(jax.random.fold_in(jax.random.fold_in(own_key, 6), dim), (blocks,), jnp.float32, least / len(split), high / len(split))
        gain = gain * jnp.repeat(jnp.exp(draws), extent[dim] // blocks).reshape((-1,) + (1,) * (len(extent) - 1 - dim))
    return gain


def noise(rng, dims, spread, most, cuts=(), dtype=jnp.bfloat16):
    level = levels(rng, dims, cuts, -0.22, 0.18) if cuts else 1.0
    values = jax.random.normal(rng, dims, jnp.float32) * spread * level
    return jnp.minimum(jnp.maximum(values, -most), most).astype(dtype)


def setup_inputs(seed: int = 0) -> dict:
    seeds = jax.random.split(jax.random.key(seed), 8)
    return {
        "image": noise(seeds[0], (C1, NXH, DEPTH, NYH), 1.0, 6.0, ((1, 64), (3, 4))),
        "w_first": noise(seeds[1], (C1, C1, 3, 3, 3), (27 * C1) ** -0.5, 0.21875),
        "b_first": noise(seeds[2], (C1,), 0.5, 3.0, (), jnp.float32),
        "w_second": noise(seeds[3], (C2, C1, 3, 3, 3), (27 * C1) ** -0.5, 0.21875),
        "b_second": noise(seeds[4], (C2,), 0.5, 3.0, (), jnp.float32),
        "w_third": noise(seeds[5], (C2, C2, 3, 3, 3), (27 * C2) ** -0.5, 0.15625),
        "b_third": noise(seeds[6], (C2,), 0.5, 3.0, (), jnp.float32),
    }


def convolve(values, kernel, offset):
    summed = lax.conv_general_dilated(values[None], kernel, (1, 1, 1), "SAME", dimension_numbers=("NCDHW", "OIDHW", "NCDHW"), preferred_element_type=jnp.float32)[0]
    return jnp.maximum(summed + offset[:, None, None, None], 0.0)


def max_pool(values):
    chans, inline, depth, cross = values.shape
    blocks = values.reshape(chans, inline // 2, 2, depth // 2, 2, cross // 2, 2)
    return jnp.max(blocks, axis=(2, 4, 6))


def reference(image, w_first, b_first, w_second, b_second, w_third, b_third):
    layer_one = convolve(image, w_first, b_first).astype(jnp.bfloat16)
    pooled = max_pool(layer_one)
    second = convolve(pooled, w_second, b_second).astype(jnp.bfloat16)
    return convolve(second, w_third, b_third).astype(jnp.bfloat16)
```

```python
import functools

import jax
import jax.numpy as jnp
from jax import lax
from jax.experimental import pallas as pl
from jax.experimental.pallas import tpu as pltpu
from jax.sharding import PartitionSpec as P

BF = jnp.bfloat16
F32 = jnp.float32
MESH = pl.DeviceIdType.MESH

FINE = ((0, -1), (0, 1), (-1, -1), (-1, 1), (1, -1), (1, 1))
COARSE = ((0, -1), (0, 1), (-1, 0), (-1, -1), (-1, 1), (1, 0), (1, -1), (1, 1))


def slot_of(dx, dy):
    order = {0: 0, -1: 1, 1: 2}
    return 3 * order[dx] + order[dy]


def iota(shape, dim):
    return lax.broadcasted_iota(jnp.int32, shape, dim)


def onehot(cond):
    return jnp.where(cond, 1.0, 0.0).astype(BF)


def mm(a, b):
    return jnp.dot(a, b, preferred_element_type=F32)


def mm_tn(a, b):
    return lax.dot_general(a, b, (((0,), (0,)), ((), ())), preferred_element_type=F32)


def mm_nt(a, b):
    return lax.dot_general(a, b, (((1,), (1,)), ((), ())), preferred_element_type=F32)


def build_banded(u_ref, t_ref, chans, lanes, depth, parities):
    row = iota((8, 128), 0)
    z_in = iota((8, 128), 1) % depth

    def tap(k, carry):
        a, f = k // 3, k % 3
        for par in range(parities):
            masks = [z_in == parities * row + par + e - 1 for e in range(3)]
            for pair in range(chans // 2):
                for lt in range(lanes // 128):
                    halves = []
                    for o in (2 * pair, 2 * pair + 1):
                        value = jnp.zeros((8, 128), F32)
                        for e in range(3):
                            line = u_ref[(a * 3 + e) * 3 + f, o:o + 1, lt * 128:(lt + 1) * 128]
                            value = jnp.where(masks[e], jnp.broadcast_to(line, (8, 128)), value)
                        halves.append(value)
                    block = jnp.concatenate(halves, axis=0).astype(BF)
                    top = par * chans * 8 + pair * 16
                    t_ref[top:top + 16, pl.ds(pl.multiple_of(k * lanes + lt * 128, 128), 128)] = block
        return carry

    lax.fori_loop(0, 9, tap, 0)


def kernel(nx, ny, image, w1, b1, w2, b2, w3, b3, out,
           x_v, w1_v, w2_v, w3_v, u1, u2, u3, t1, t2, t3, bb, acc, split, fine_pk, own_pk,
           sel, p_own, p_left, p_right, coarse_pk, own_pk2, p3, s_v, s3, bias1, bias2, bias3,
           local_sems, send_x, recv_x, send_f, recv_f, send_p, recv_p, send_c, recv_c):
    gx, gy = lax.axis_index("gx"), lax.axis_index("gy")

    def at(dx, dy):
        return (lax.rem(gx + dx + nx, nx), lax.rem(gy + dy + ny, ny))

    first_x, last_x = gx == 0, gx == nx - 1
    first_y, last_y = gy == 0, gy == ny - 1

    loads = [pltpu.make_async_copy(image.at[:, r], x_v.at[r + 1], local_sems.at[r]) for r in range(4)]
    loads += [pltpu.make_async_copy(src, dst, local_sems.at[4 + i])
              for i, (src, dst) in enumerate(((w1, w1_v), (w2, w2_v), (w3, w3_v)))]
    for load in loads:
        load.start()

    barrier = pltpu.get_barrier_semaphore()
    for d in COARSE:
        pl.semaphore_signal(barrier, inc=1, device_id=at(*d), device_id_type=MESH)

    for load in loads[:4]:
        load.wait()
    ends = jnp.zeros((16, 512), F32)
    r16, l16 = iota((16, 256), 0), iota((16, 256), 1)
    for r in range(4):
        pick = onehot(((r16 == 2 * r) & (l16 == 0)) | ((r16 == 2 * r + 1) & (l16 == 255)))
        ends = ends + mm_nt(pick, x_v[r + 1].reshape(512, 256))
    own_pk[...] = ends.astype(BF)

    pl.semaphore_wait(barrier, len(COARSE))

    rows_x = []
    for i, (r, dst, dx) in enumerate(((0, 5, -1), (3, 0, 1))):
        rows_x.append(pltpu.make_async_remote_copy(
            src_ref=image.at[:, r], dst_ref=x_v.at[dst], send_sem=send_x.at[i], recv_sem=recv_x.at[i],
            device_id=at(dx, 0), device_id_type=MESH))
    for copy in rows_x:
        copy.start()
    fine = {}
    for i, d in enumerate(FINE):
        back = FINE.index((-d[0], -d[1]))
        fine[d] = pltpu.make_async_remote_copy(
            src_ref=own_pk, dst_ref=fine_pk.at[back], send_sem=send_f.at[i], recv_sem=recv_f.at[back],
            device_id=at(*d), device_id_type=MESH)
        fine[d].start()

    for k, (src, dst, n) in enumerate(((b1, bias1, 32), (b2, bias2, 64), (b3, bias3, 64))):
        for o in range(n):
            dst[o * 8:(o + 1) * 8, :] = jnp.full((8, 128), src[o], F32)

    for load in loads[4:]:
        load.wait()
    q1 = onehot(iota((32, 512), 1) // 16 == iota((32, 512), 0))
    u1[...] = mm(w1_v[...].reshape(864, 32), q1).reshape(27, 32, 512)
    build_banded(u1, t1, 32, 512, 16, 2)

    sy, sl = iota((256, 512), 0), iota((256, 512), 1)
    part, pos = sl // 128, sl % 128
    split[...] = onehot(sy == 2 * pos + part - 1)

    def stack_row(i, pack, left, right, keep):
        d = mm(x_v[i].reshape(512, 256), split[...])
        r32, l32 = iota((32, 256), 0), iota((32, 256), 1)
        pick = onehot(((r32 == left) & (l32 == 0)) | ((r32 == right) & (l32 == 255)))
        h = mm_tn(pack, pick)
        odd_before = d[:, :128] + h[:, :128]
        even_after = d[:, 384:] + h[:, 128:]
        full = jnp.concatenate([odd_before, d[:, 128:384], even_after], axis=1)
        if keep is not None:
            full = full * keep
        full = full.astype(BF)
        for f in range(3):
            start = i * 1536 + f * 512
            if not isinstance(start, int):
                start = pl.multiple_of(start, 512)
            bb[pl.ds(start, 512), :] = full[:, f * 128:f * 128 + 256]

    fine[(0, 1)].wait_recv()
    fine[(0, -1)].wait_recv()

    def own_row(i, carry):
        left = jnp.where(first_y, -1, 2 * (i - 1) + 1)
        right = jnp.where(last_y, -1, 16 + 2 * (i - 1))
        stack_row(i, fine_pk[0:2].reshape(32, 512), left, right, None)
        return carry

    lax.fori_loop(1, 5, own_row, 0)

    acc[0] = mm(t1[:, 1536:], bb[1536:4608, :])

    def middle(i, carry):
        acc[i] = mm(t1[...], bb[pl.ds(pl.multiple_of(i * 1536, 512), 4608), :])
        return carry

    lax.fori_loop(1, 3, middle, 0)
    acc[3] = mm(t1[:, :3072], bb[4608:7680, :])

    for tap in range(27):
        q2 = onehot(iota((32, 256), 1) // 8 == iota((32, 256), 0))
        u2[tap] = mm_tn(w2_v[tap], q2)
    build_banded(u2, t2, 64, 256, 8, 1)
    q3 = onehot(iota((64, 512), 1) // 8 == iota((64, 512), 0))
    u3[...] = mm(w3_v[...].reshape(1728, 64), q3).reshape(27, 64, 512)
    build_banded(u3, t3, 64, 512, 8, 1)

    r144 = iota((144, 256), 0)
    l144 = iota((144, 256), 1)
    for jj in range(6):
        dx, j = ((-1, 0, 1)[jj // 2], jj % 2)
        left = slot_of(dx, -1) * 16 + j * 4 + 3
        right = slot_of(dx, 1) * 16 + j * 4
        sel[:, jj * 256:(jj + 1) * 256] = onehot(
            ((r144 == left) & (l144 == 0)) | ((r144 == right) & (l144 == 255)))
    re, le = iota((144, 128), 0), iota((144, 128), 1)
    xo, side = le // 2, le % 2
    for a in range(3):
        jj = xo + a
        group = jnp.where(jj < 2, 1, jnp.where(jj < 4, 0, 2))
        for f in range(3):
            dyl, cil = ((1, 2), (1, 3), (0, 0))[f]
            dyr, cir = ((0, 3), (2, 0), (2, 1))[f]
            want = jnp.where(side == 0, dyl * 16 + cil, dyr * 16 + cir) + group * 48 + (jj % 2) * 4
            tile = 1536 + (a * 3 + f) * 128
            sel[:, tile:tile + 128] = onehot((re == want) & (le < 8))

    def from_side(i, dx, copy):
        copy.wait_recv()
        fine[(-dx, 1)].wait_recv()
        fine[(-dx, -1)].wait_recv()
        edge = first_x if dx < 0 else last_x
        r = 3 if dx < 0 else 0
        left = jnp.where(first_y, -1, 2 * r + 1)
        right = jnp.where(last_y, -1, 16 + 2 * r)
        base = 2 if dx < 0 else 4
        stack_row(i, fine_pk[base:base + 2].reshape(32, 512), left, right, jnp.where(edge, 0.0, 1.0))

    def pool(x):
        m = jnp.maximum(acc[2 * x], acc[2 * x + 1])
        m = jnp.maximum(m[:, :128], m[:, 128:])
        m = jnp.maximum(m[:256], m[256:])
        p_own[x] = jnp.maximum(m + bias1[...], 0.0).astype(BF)

    from_side(0, -1, rows_x[1])
    acc[0] += mm(t1[:, :1536], bb[0:1536, :])
    pool(0)
    from_side(5, 1, rows_x[0])
    acc[3] += mm(t1[:, 3072:], bb[7680:9216, :])
    pool(1)

    rows_p = []
    for i, (dst, dx) in enumerate(((p_right, -1), (p_left, 1))):
        rows_p.append(pltpu.make_async_remote_copy(
            src_ref=p_own, dst_ref=dst, send_sem=send_p.at[i], recv_sem=recv_p.at[i],
            device_id=at(dx, 0), device_id_type=MESH))
    for copy in rows_p:
        copy.start()
    ends = jnp.zeros((16, 256), F32)
    r16, l16 = iota((16, 128), 0), iota((16, 128), 1)
    for j in range(2):
        pick = onehot((r16 // 4 == j) & (l16 == jnp.where(r16 % 4 < 2, r16 % 4, 124 + r16 % 4)))
        ends = ends + mm_nt(pick, p_own[j])
    own_pk2[...] = ends.astype(BF)
    coarse = {}
    for i, d in enumerate(COARSE):
        back = COARSE.index((-d[0], -d[1]))
        coarse[d] = pltpu.make_async_remote_copy(
            src_ref=own_pk2, dst_ref=coarse_pk.at[slot_of(-d[0], -d[1])], send_sem=send_c.at[i],
            recv_sem=recv_c.at[back], device_id=at(*d), device_id_type=MESH)
        coarse[d].start()
    coarse_pk[0] = ends.astype(BF)

    for copy in coarse.values():
        copy.wait_recv()
    rr = iota((144, 256), 0) // 16
    gone_x = ((rr // 3 == 1) & first_x) | ((rr // 3 == 2) & last_x)
    gone_y = ((rr % 3 == 1) & first_y) | ((rr % 3 == 2) & last_y)
    packs = coarse_pk[...].reshape(144, 256)
    packs = jnp.where(gone_x | gone_y, 0.0, packs.astype(F32)).astype(BF)
    h = mm_tn(packs, sel[...])
    for k in range(9):
        p3[k * 256:(k + 1) * 256, 512:640] = h[:, 1536 + k * 128:1664 + k * 128].astype(BF)

    ys, js = iota((128, 256), 0), iota((128, 256), 1)
    shift = onehot(ys == jnp.where(js < 128, js - 1, js - 127))

    def place(jj, p):
        g = (mm(p, shift) + h[:, jj * 256:(jj + 1) * 256]).astype(BF)
        parts = (g[:, :128], p, g[:, 128:])
        for a in range(3):
            if 0 <= jj - a < 4:
                for f in range(3):
                    top = (a * 3 + f) * 256
                    p3[top:top + 256, (jj - a) * 128:(jj - a + 1) * 128] = parts[f]

    place(2, p_own[0])
    place(3, p_own[1])
    for copy, src, base, edge in ((rows_p[1], p_left, 0, first_x), (rows_p[0], p_right, 4, last_x)):
        copy.wait_recv()
        keep = jnp.where(edge, 0.0, 1.0)
        for j in range(2):
            place(base + j, (src[j].astype(F32) * keep).astype(BF))

    lane = iota((1, 640), 1)
    tile, low = lane // 128, lane % 128
    row = jnp.where(tile < 4, tile, low // 2)
    gone = ((row == 0) & first_x) | ((row == 3) & last_x)
    gone = gone | ((tile == 4) & (((low % 2 == 0) & first_y) | ((low % 2 == 1) & last_y)))
    keep = jnp.where(gone, 0.0, 1.0)
    s = mm(t2[...], p3[...])
    s = jnp.maximum(s + jnp.concatenate([bias2[...]] * 5, axis=1), 0.0) * keep
    s_v[...] = s.astype(BF)

    ye, je = iota((128, 256), 0), iota((128, 256), 1)
    for x in range(4):
        mid = s_v[:, x * 128:(x + 1) * 128]
        pick = onehot(((ye == 2 * x) & (je == 0)) | ((ye == 2 * x + 1) & (je == 255)))
        both = jnp.concatenate([mid, s_v[:, 512:640]], axis=1)
        g = mm(both, jnp.concatenate([shift, pick], axis=0)).astype(BF)
        parts = (g[:, :128], mid, g[:, 128:])
        for a in range(3):
            if 0 <= x - a < 2:
                for f in range(3):
                    top = (a * 3 + f) * 512
                    s3[top:top + 512, (x - a) * 128:(x - a + 1) * 128] = parts[f]

    c = mm(t3[...], s3[...])
    c = jnp.maximum(c + jnp.concatenate([bias3[...]] * 2, axis=1), 0.0)
    for x in range(2):
        out[:, x] = c[:, x * 128:(x + 1) * 128].reshape(64, 8, 128).astype(BF)

    for copy in rows_x + list(fine.values()) + rows_p + list(coarse.values()):
        copy.wait_send()


def per_device(image, w_first, b_first, w_second, b_second, w_third, b_third):
    nx, ny = lax.axis_size("gx"), lax.axis_size("gy")
    w1 = jnp.transpose(w_first, (2, 3, 4, 0, 1)).reshape(27, 32, 32)
    w2 = jnp.transpose(w_second, (2, 3, 4, 1, 0)).reshape(27, 32, 64)
    w3 = jnp.transpose(w_third, (2, 3, 4, 0, 1)).reshape(27, 64, 64)
    anywhere = pl.BlockSpec(memory_space=pl.ANY)
    scalars = pl.BlockSpec(memory_space=pltpu.SMEM)
    dma = pltpu.SemaphoreType.DMA
    return pl.pallas_call(
        functools.partial(kernel, nx, ny),
        out_shape=jax.ShapeDtypeStruct((64, 2, 8, 128), BF),
        in_specs=[anywhere, anywhere, scalars, anywhere, scalars, anywhere, scalars],
        out_specs=pl.BlockSpec(memory_space=pltpu.VMEM),
        scratch_shapes=[
            pltpu.VMEM((6, 32, 16, 256), BF),
            pltpu.VMEM((27, 32, 32), BF),
            pltpu.VMEM((27, 32, 64), BF),
            pltpu.VMEM((27, 64, 64), BF),
            pltpu.VMEM((27, 32, 512), F32),
            pltpu.VMEM((27, 64, 256), F32),
            pltpu.VMEM((27, 64, 512), F32),
            pltpu.VMEM((512, 4608), BF),
            pltpu.VMEM((512, 2304), BF),
            pltpu.VMEM((512, 4608), BF),
            pltpu.VMEM((9216, 256), BF),
            pltpu.VMEM((4, 512, 256), F32),
            pltpu.VMEM((256, 512), BF),
            pltpu.VMEM((6, 16, 512), BF),
            pltpu.VMEM((16, 512), BF),
            pltpu.VMEM((144, 2688), BF),
            pltpu.VMEM((2, 256, 128), BF),
            pltpu.VMEM((2, 256, 128), BF),
            pltpu.VMEM((2, 256, 128), BF),
            pltpu.VMEM((9, 16, 256), BF),
            pltpu.VMEM((16, 256), BF),
            pltpu.VMEM((2304, 640), BF),
            pltpu.VMEM((512, 640), BF),
            pltpu.VMEM((4608, 256), BF),
            pltpu.VMEM((256, 128), F32),
            pltpu.VMEM((512, 128), F32),
            pltpu.VMEM((512, 128), F32),
            dma((7,)), dma((2,)), dma((2,)), dma((6,)), dma((6,)),
            dma((2,)), dma((2,)), dma((8,)), dma((8,)),
        ],
        compiler_params=pltpu.CompilerParams(
            collective_id=0, has_side_effects=True, vmem_limit_bytes=60 * 1024 * 1024),
        name="encoder",
    )(image, w1, b_first, w2, b_second, w3, b_third)


def solution(mesh):
    placed = (P(None, "gx", None, "gy"), P(), P(), P(), P(), P(), P())
    return jax.shard_map(
        per_device, mesh=mesh, in_specs=placed, out_specs=P(None, "gx", None, "gy"), check_vma=False
    )
```

```python
import functools

import jax
import jax.numpy as jnp
from jax import lax
from jax.experimental import pallas as pl
from jax.experimental.pallas import tpu as pltpu
from jax.sharding import PartitionSpec as P

BF = jnp.bfloat16
F32 = jnp.float32
MESH = pl.DeviceIdType.MESH

FINE = ((0, -1), (0, 1), (-1, -1), (-1, 1), (1, -1), (1, 1))
COARSE = ((0, -1), (0, 1), (-1, 0), (-1, -1), (-1, 1), (1, 0), (1, -1), (1, 1))


def slot_of(dx, dy):
    order = {0: 0, -1: 1, 1: 2}
    return 3 * order[dx] + order[dy]


def iota(shape, dim):
    return lax.broadcasted_iota(jnp.int32, shape, dim)


def onehot(cond):
    return jnp.where(cond, 1.0, 0.0).astype(BF)


def mm(a, b):
    return jnp.dot(a, b, preferred_element_type=F32)


def mm_tn(a, b):
    return lax.dot_general(a, b, (((0,), (0,)), ((), ())), preferred_element_type=F32)


def mm_nt(a, b):
    return lax.dot_general(a, b, (((1,), (1,)), ((), ())), preferred_element_type=F32)


def build_banded(u_ref, t_ref, chans, lanes, depth, parities, groups):
    row = iota((8, 128), 0)
    z_in = iota((8, 128), 1) % depth

    def tap(k, carry):
        a, f = k // 3, k % 3
        for par in range(parities):
            masks = [z_in == parities * row + par + e - 1 for e in range(3)]
            for pair in range(chans // 2):
                for lt in range(lanes // 128):
                    halves = []
                    for o in (2 * pair, 2 * pair + 1):
                        value = jnp.zeros((8, 128), F32)
                        for e in range(3):
                            line = u_ref[(a * 3 + e) * 3 + f, o:o + 1, lt * 128:(lt + 1) * 128]
                            value = jnp.where(masks[e], jnp.broadcast_to(line, (8, 128)), value)
                        halves.append(value)
                    block = jnp.concatenate(halves, axis=0).astype(BF)
                    top = par * chans * 8 + pair * 16
                    part = lanes // groups
                    group, rest = lt * 128 // part, lt * 128 % part
                    lane = a * (3 * lanes) + f * part + (group * 3 * part + rest)
                    t_ref[top:top + 16, pl.ds(pl.multiple_of(lane, 128), 128)] = block
        return carry

    lax.fori_loop(0, 9, tap, 0)


def kernel(nx, ny, image, w1, b1, w2, b2, w3, b3, out,
           x_v, w1_v, w2_v, w3_v, u1, u2, u3, t1, t2, t3, bb, acc, split, shift, fine_pk, own_pk,
           sel, p_own, p_left, p_right, coarse_pk, own_pk2, p_mid, p_lo, p_hi, p_mix, p_edge, s_acc, s_v, s3,
           bias1, bias2, bias3, b1_s, b2_s, b3_s,
           local_sems, send_x, recv_x, send_f, recv_f, send_p, recv_p, send_c, recv_c):
    gx, gy = lax.axis_index("gx"), lax.axis_index("gy")

    def at(dx, dy):
        return (lax.rem(gx + dx + nx, nx), lax.rem(gy + dy + ny, ny))

    first_x, last_x = gx == 0, gx == nx - 1
    first_y, last_y = gy == 0, gy == ny - 1

    barrier = pltpu.get_barrier_semaphore()
    for d in COARSE:
        pl.semaphore_signal(barrier, inc=1, device_id=at(*d), device_id_type=MESH)

    loads = [pltpu.make_async_copy(w1, w1_v, local_sems.at[0])]
    loads += [pltpu.make_async_copy(image.at[:, r], x_v.at[r + 1], local_sems.at[r + 1]) for r in range(4)]
    loads += [pltpu.make_async_copy(src, dst, local_sems.at[5 + i]) for i, (src, dst) in enumerate(
        ((w2, w2_v), (w3, w3_v), (b1, b1_s), (b2, b2_s), (b3, b3_s)))]
    for load in loads:
        load.start()

    loads[0].wait()
    q1 = onehot(iota((32, 512), 1) // 16 == iota((32, 512), 0))
    u1[...] = mm(w1_v[...].reshape(864, 32), q1).reshape(27, 32, 512)
    build_banded(u1, t1, 32, 512, 16, 2, 2)

    for load in loads[1:5]:
        load.wait()
    ends = jnp.zeros((16, 512), F32)
    r16, l16 = iota((16, 256), 0), iota((16, 256), 1)
    for r in range(4):
        pick = onehot(((r16 == 2 * r) & (l16 == 0)) | ((r16 == 2 * r + 1) & (l16 == 255)))
        ends = ends + mm_nt(pick, x_v[r + 1].reshape(512, 256))
    own_pk[...] = ends.astype(BF)

    pl.semaphore_wait(barrier, len(COARSE))

    fine = {}
    for i, d in enumerate(FINE):
        back = FINE.index((-d[0], -d[1]))
        fine[d] = pltpu.make_async_remote_copy(
            src_ref=own_pk, dst_ref=fine_pk.at[back], send_sem=send_f.at[i], recv_sem=recv_f.at[back],
            device_id=at(*d), device_id_type=MESH)
        fine[d].start()

    def row_copy(i, h):
        r, dst, dx = ((0, 5, -1), (3, 0, 1))[i]
        chans = pl.ds(h * 16, 16)
        return pltpu.make_async_remote_copy(
            src_ref=image.at[chans, r], dst_ref=x_v.at[dst, chans], send_sem=send_x.at[i, h],
            recv_sem=recv_x.at[i, h], device_id=at(dx, 0), device_id_type=MESH)

    for h in range(2):
        for i in range(2):
            row_copy(i, h).start()

    for load in loads[5:]:
        load.wait()
    for src, dst, n in ((b1_s, bias1, 32), (b2_s, bias2, 64), (b3_s, bias3, 64)):
        for o in range(n):
            dst[o * 8:(o + 1) * 8, :] = jnp.full((8, 128), src[o], F32)

    q2 = onehot(iota((32, 256), 1) // 8 == iota((32, 256), 0))
    for tap in range(27):
        u2[tap] = mm_tn(w2_v[tap], q2)
    build_banded(u2, t2, 64, 256, 8, 1, 1)

    sy, sl = iota((256, 512), 0), iota((256, 512), 1)
    split[...] = onehot(sy == 2 * (sl % 128) + sl // 128 - 1)
    ys, js = iota((128, 256), 0), iota((128, 256), 1)
    shift[...] = onehot(ys == jnp.where(js < 128, js - 1, js - 127))

    def stack(i, h, pack, left, right, keep):
        d = mm(x_v[i, pl.ds(h * 16, 16)].reshape(256, 256), split[...])
        r32, l32 = iota((32, 256), 0), iota((32, 256), 1)
        pick = onehot(((r32 == left) & (l32 == 0)) | ((r32 == right) & (l32 == 255)))
        e = mm_tn(pack, pick)
        full = jnp.concatenate([d[:, :128] + e[:, :128], d[:, 128:384], d[:, 384:] + e[:, 128:]], axis=1)
        if keep is not None:
            full = full * keep
        full = full.astype(BF)
        for f in range(3):
            start = pl.multiple_of(i * 1536 + h * 768 + f * 256, 256)
            bb[pl.ds(start, 256), :] = full[:, f * 128:f * 128 + 256]

    fine[(0, 1)].wait_recv()
    fine[(0, -1)].wait_recv()

    def own_row(i, carry):
        left = jnp.where(first_y, -1, 2 * (i - 1) + 1)
        right = jnp.where(last_y, -1, 16 + 2 * (i - 1))
        for h in range(2):
            stack(i, h, fine_pk[0:2, :, h * 256:(h + 1) * 256].reshape(32, 256), left, right, None)
        return carry

    lax.fori_loop(1, 5, own_row, 0)

    acc[0] = mm(t1[:, 1536:], bb[1536:4608, :])
    acc[3] = mm(t1[:, :3072], bb[4608:7680, :])

    def middle(i, carry):
        acc[i] = mm(t1[...], bb[pl.ds(pl.multiple_of(i * 1536, 512), 4608), :])
        return carry

    lax.fori_loop(1, 3, middle, 0)

    q3 = onehot(iota((64, 512), 1) // 8 == iota((64, 512), 0))
    u3[...] = mm(w3_v[...].reshape(1728, 64), q3).reshape(27, 64, 512)
    build_banded(u3, t3, 64, 512, 8, 1, 1)

    r144 = iota((144, 256), 0)
    l144 = iota((144, 256), 1)
    for jj in range(6):
        dx, j = ((-1, 0, 1)[jj // 2], jj % 2)
        left = slot_of(dx, -1) * 16 + j * 4 + 3
        right = slot_of(dx, 1) * 16 + j * 4
        sel[:, jj * 256:(jj + 1) * 256] = onehot(
            ((r144 == left) & (l144 == 0)) | ((r144 == right) & (l144 == 255)))
    re, le = iota((144, 128), 0), iota((144, 128), 1)
    xo, side = le // 2, le % 2
    for a in range(3):
        jj = xo + a
        group = jnp.where(jj < 2, 1, jnp.where(jj < 4, 0, 2))
        for f in range(3):
            dyl, cil = ((1, 2), (1, 3), (0, 0))[f]
            dyr, cir = ((0, 3), (2, 0), (2, 1))[f]
            want = jnp.where(side == 0, dyl * 16 + cil, dyr * 16 + cir) + group * 48 + (jj % 2) * 4
            tile = 1536 + (a * 3 + f) * 128
            sel[:, tile:tile + 128] = onehot((re == want) & (le < 8))

    for d in FINE[2:]:
        fine[d].wait_recv()

    def halo_half(h, carry):
        for i, row, base, r, edge in ((1, 0, 2, 3, first_x), (0, 5, 4, 0, last_x)):
            row_copy(i, h).wait_recv()
            left = jnp.where(first_y, -1, 2 * r + 1)
            right = jnp.where(last_y, -1, 16 + 2 * r)
            pack = fine_pk[base:base + 2, :, pl.ds(pl.multiple_of(h * 256, 256), 256)].reshape(32, 256)
            stack(row, h, pack, left, right, jnp.where(edge, 0.0, 1.0))
        k = pl.multiple_of(h * 768, 256)
        acc[0] += mm(t1[:, pl.ds(k, 768)], bb[pl.ds(k, 768), :])
        acc[3] += mm(t1[:, pl.ds(3072 + k, 768)], bb[pl.ds(7680 + k, 768), :])
        return carry

    lax.fori_loop(0, 2, halo_half, 0)

    def pooled_copy(i, j):
        dst, dx = ((p_right, -1), (p_left, 1))[i]
        return pltpu.make_async_remote_copy(
            src_ref=p_own.at[j], dst_ref=dst.at[j], send_sem=send_p.at[i, j], recv_sem=recv_p.at[i, j],
            device_id=at(dx, 0), device_id_type=MESH)

    for j in range(2):
        m = jnp.maximum(acc[2 * j], acc[2 * j + 1])
        m = jnp.maximum(m[:, :128], m[:, 128:])
        m = jnp.maximum(m[:256], m[256:])
        p_own[j] = jnp.maximum(m + bias1[...], 0.0).astype(BF)
        for i in range(2):
            pooled_copy(i, j).start()

    ends = jnp.zeros((16, 256), F32)
    r16, l16 = iota((16, 128), 0), iota((16, 128), 1)
    for j in range(2):
        pick = onehot((r16 // 4 == j) & (l16 == jnp.where(r16 % 4 < 2, r16 % 4, 124 + r16 % 4)))
        ends = ends + mm_nt(pick, p_own[j])
    own_pk2[...] = ends.astype(BF)
    coarse = {}
    for i, d in enumerate(COARSE):
        back = COARSE.index((-d[0], -d[1]))
        coarse[d] = pltpu.make_async_remote_copy(
            src_ref=own_pk2, dst_ref=coarse_pk.at[slot_of(-d[0], -d[1])], send_sem=send_c.at[i],
            recv_sem=recv_c.at[back], device_id=at(*d), device_id_type=MESH)
        coarse[d].start()
    coarse_pk[0] = ends.astype(BF)

    def known(packs, n):
        rr = iota((n, 256), 0) // 16
        gone_x = ((rr // 3 == 1) & first_x) | ((rr // 3 == 2) & last_x)
        gone_y = ((rr % 3 == 1) & first_y) | ((rr % 3 == 2) & last_y)
        return jnp.where(gone_x | gone_y, 0.0, packs.astype(F32)).astype(BF)

    def place(p, ends, spots):
        g = (mm(p, shift[...]) + ends).astype(BF)
        parts = (g[:, :128], p, g[:, 128:])
        for ref, half in spots:
            for f in range(3):
                ref[f * 256:(f + 1) * 256, half * 128:(half + 1) * 128] = parts[f]

    coarse[(0, 1)].wait_recv()
    coarse[(0, -1)].wait_recv()
    e = mm_tn(known(coarse_pk[0:3].reshape(48, 256), 48), sel[0:48, 512:1024])
    place(p_own[0], e[:, :256], ((p_mid, 0),))
    place(p_own[1], e[:, 256:], ((p_mid, 1),))

    def own_second(m, carry):
        rows = pl.ds(pl.multiple_of(m * 256, 256), 256)
        parts = [mm(t2[rows, a * 768:(a + 1) * 768], p_mid[...]) for a in range(3)]
        s_acc[rows, 0:128] = parts[2][:, :128]
        s_acc[rows, 128:256] = parts[2][:, 128:] + parts[1][:, :128]
        s_acc[rows, 256:384] = parts[1][:, 128:] + parts[0][:, :128]
        s_acc[rows, 384:512] = parts[0][:, 128:]
        return carry

    lax.fori_loop(0, 2, own_second, 0)

    for d in COARSE[2:]:
        coarse[d].wait_recv()
    e = mm_tn(known(coarse_pk[...].reshape(144, 256), 144), sel[...])
    for k in range(9):
        p_edge[k * 256:(k + 1) * 256, :] = e[:, 1536 + k * 128:1664 + k * 128].astype(BF)
    for j in range(2):
        for i, src, base, edge in ((1, p_left, 0, first_x), (0, p_right, 4, last_x)):
            pooled_copy(i, j).wait_recv()
            jj = base + j
            spots = {0: ((p_lo, 0),), 1: ((p_lo, 1), (p_mix, 0)), 4: ((p_mix, 1), (p_hi, 0)), 5: ((p_hi, 1),)}[jj]
            p = (src[j].astype(F32) * jnp.where(edge, 0.0, 1.0)).astype(BF)
            place(p, e[:, jj * 256:(jj + 1) * 256], spots)

    lane = iota((1, 640), 1)
    tile, low = lane // 128, lane % 128
    row = jnp.where(tile < 4, tile, low // 2)
    gone = ((row == 0) & first_x) | ((row == 3) & last_x)
    gone = gone | ((tile == 4) & (((low % 2 == 0) & first_y) | ((low % 2 == 1) & last_y)))
    keep = jnp.where(gone, 0.0, 1.0)

    def second(m, carry):
        rows = pl.ds(pl.multiple_of(m * 256, 256), 256)
        lo = mm(t2[rows, 0:768], p_lo[...])
        mix = mm(t2[rows, 768:1536], p_mix[...])
        hi = mm(t2[rows, 1536:2304], p_hi[...])
        edge = mm(t2[rows, :], p_edge[...])
        added = (lo[:, :128] + mix[:, :128], lo[:, 128:], hi[:, :128], mix[:, 128:] + hi[:, 128:])
        for t in range(5):
            cut = slice(t * 128, (t + 1) * 128)
            total = edge if t == 4 else s_acc[rows, cut] + added[t]
            s_v[rows, cut] = (jnp.maximum(total + bias2[rows, :], 0.0) * keep[:, cut]).astype(BF)
        return carry

    lax.fori_loop(0, 2, second, 0)

    ye, je = iota((128, 256), 0), iota((128, 256), 1)
    for x in range(4):
        mid = s_v[:, x * 128:(x + 1) * 128]
        pick = onehot(((ye == 2 * x) & (je == 0)) | ((ye == 2 * x + 1) & (je == 255)))
        both = jnp.concatenate([mid, s_v[:, 512:640]], axis=1)
        g = mm(both, jnp.concatenate([shift[...], pick], axis=0)).astype(BF)
        parts = (g[:, :128], mid, g[:, 128:])
        for a in range(3):
            if 0 <= x - a < 2:
                for f in range(3):
                    top = (a * 3 + f) * 512
                    s3[top:top + 512, (x - a) * 128:(x - a + 1) * 128] = parts[f]

    def third(m, carry):
        rows = pl.ds(pl.multiple_of(m * 256, 256), 256)
        c = mm(t3[rows, :], s3[...])
        for x in range(2):
            block = jnp.maximum(c[:, x * 128:(x + 1) * 128] + bias3[rows, :], 0.0)
            out[pl.ds(m * 32, 32), x] = block.reshape(32, 8, 128).astype(BF)
        return carry

    lax.fori_loop(0, 2, third, 0)

    for i in range(2):
        for h in range(2):
            row_copy(i, h).wait_send()
            pooled_copy(i, h).wait_send()
    for copy in list(fine.values()) + list(coarse.values()):
        copy.wait_send()


def per_device(image, w_first, b_first, w_second, b_second, w_third, b_third):
    nx, ny = lax.axis_size("gx"), lax.axis_size("gy")
    w1 = jnp.transpose(w_first, (2, 3, 4, 0, 1)).reshape(27, 32, 32)
    w2 = jnp.transpose(w_second, (2, 3, 4, 1, 0)).reshape(27, 32, 64)
    w3 = jnp.transpose(w_third, (2, 3, 4, 0, 1)).reshape(27, 64, 64)
    anywhere = pl.BlockSpec(memory_space=pltpu.HBM)
    dma = pltpu.SemaphoreType.DMA
    return pl.pallas_call(
        functools.partial(kernel, nx, ny),
        out_shape=jax.ShapeDtypeStruct((64, 2, 8, 128), BF),
        in_specs=[anywhere] * 7,
        out_specs=pl.BlockSpec(memory_space=pltpu.VMEM),
        scratch_shapes=[
            pltpu.VMEM((6, 32, 16, 256), BF),
            pltpu.VMEM((27, 32, 32), BF),
            pltpu.VMEM((27, 32, 64), BF),
            pltpu.VMEM((27, 64, 64), BF),
            pltpu.VMEM((27, 32, 512), F32),
            pltpu.VMEM((27, 64, 256), F32),
            pltpu.VMEM((27, 64, 512), F32),
            pltpu.VMEM((512, 4608), BF),
            pltpu.VMEM((512, 2304), BF),
            pltpu.VMEM((512, 4608), BF),
            pltpu.VMEM((9216, 256), BF),
            pltpu.VMEM((4, 512, 256), F32),
            pltpu.VMEM((256, 512), BF),
            pltpu.VMEM((128, 256), BF),
            pltpu.VMEM((6, 16, 512), BF),
            pltpu.VMEM((16, 512), BF),
            pltpu.VMEM((144, 2688), BF),
            pltpu.VMEM((2, 256, 128), BF),
            pltpu.VMEM((2, 256, 128), BF),
            pltpu.VMEM((2, 256, 128), BF),
            pltpu.VMEM((9, 16, 256), BF),
            pltpu.VMEM((16, 256), BF),
            pltpu.VMEM((768, 256), BF),
            pltpu.VMEM((768, 256), BF),
            pltpu.VMEM((768, 256), BF),
            pltpu.VMEM((768, 256), BF),
            pltpu.VMEM((2304, 128), BF),
            pltpu.VMEM((512, 512), F32),
            pltpu.VMEM((512, 640), BF),
            pltpu.VMEM((4608, 256), BF),
            pltpu.VMEM((256, 128), F32),
            pltpu.VMEM((512, 128), F32),
            pltpu.VMEM((512, 128), F32),
            pltpu.SMEM((32,), F32),
            pltpu.SMEM((64,), F32),
            pltpu.SMEM((64,), F32),
            dma((10,)), dma((2, 2)), dma((2, 2)), dma((6,)), dma((6,)),
            dma((2, 2)), dma((2, 2)), dma((8,)), dma((8,)),
        ],
        compiler_params=pltpu.CompilerParams(
            collective_id=0, has_side_effects=True, vmem_limit_bytes=67043328 - 300 * 1024),
        name="encoder",
    )(image, w1, b_first, w2, b_second, w3, b_third)


def solution(mesh):
    placed = (P(None, "gx", None, "gy"), P(), P(), P(), P(), P(), P())
    return jax.shard_map(
        per_device, mesh=mesh, in_specs=placed, out_specs=P(None, "gx", None, "gy"), check_vma=False
    )
```

```python
import functools

import jax
import jax.numpy as jnp
from jax import lax
from jax.experimental import pallas as pl
from jax.experimental.pallas import tpu as pltpu
from jax.sharding import PartitionSpec as P

BF = jnp.bfloat16
F32 = jnp.float32
MESH = pl.DeviceIdType.MESH

FINE = ((0, -1), (0, 1), (-1, -1), (-1, 1), (1, -1), (1, 1))
COARSE = ((0, -1), (0, 1), (-1, 0), (-1, -1), (-1, 1), (1, 0), (1, -1), (1, 1))


def slot_of(dx, dy):
    order = {0: 0, -1: 1, 1: 2}
    return 3 * order[dx] + order[dy]


def iota(shape, dim):
    return lax.broadcasted_iota(jnp.int32, shape, dim)


def onehot(cond):
    return jnp.where(cond, 1.0, 0.0).astype(BF)


def mm(a, b):
    return jnp.dot(a, b, preferred_element_type=F32)


def mm_tn(a, b):
    return lax.dot_general(a, b, (((0,), (0,)), ((), ())), preferred_element_type=F32)


def mm_nt(a, b):
    return lax.dot_general(a, b, (((1,), (1,)), ((), ())), preferred_element_type=F32)


def build_banded(u_ref, t_ref, chans, lanes, depth, parities, groups):
    row = iota((8, 128), 0)
    z_in = iota((8, 128), 1) % depth

    def tap(k, carry):
        a, f = k // 3, k % 3
        for par in range(parities):
            masks = [z_in == parities * row + par + e - 1 for e in range(3)]
            for pair in range(chans // 2):
                for lt in range(lanes // 128):
                    halves = []
                    for o in (2 * pair, 2 * pair + 1):
                        value = jnp.zeros((8, 128), F32)
                        for e in range(3):
                            line = u_ref[(a * 3 + e) * 3 + f, o:o + 1, lt * 128:(lt + 1) * 128]
                            value = jnp.where(masks[e], jnp.broadcast_to(line, (8, 128)), value)
                        halves.append(value)
                    block = jnp.concatenate(halves, axis=0).astype(BF)
                    top = par * chans * 8 + pair * 16
                    part = lanes // groups
                    group, rest = lt * 128 // part, lt * 128 % part
                    lane = a * (3 * lanes) + f * part + (group * 3 * part + rest)
                    t_ref[top:top + 16, pl.ds(pl.multiple_of(lane, 128), 128)] = block
        return carry

    lax.fori_loop(0, 9, tap, 0)


def kernel(nx, ny, image, w1, b1, w2, b2, w3, b3, out,
           x_v, w1_v, w2_v, w3_v, u1, u2, u3, t1, t2, t3, bb, acc, split, shift, fine_pk, own_pk,
           sel, p_own, p_left, p_right, coarse_pk, own_pk2, p_mid, p_lo, p_hi, p_mix, p_edge, s_acc, s_v, s3,
           bias1, bias2, bias3, b1_s, b2_s, b3_s,
           local_sems, send_x, recv_x, send_f, recv_f, send_p, recv_p, send_c, recv_c):
    gx, gy = lax.axis_index("gx"), lax.axis_index("gy")

    def at(dx, dy):
        return (lax.rem(gx + dx + nx, nx), lax.rem(gy + dy + ny, ny))

    first_x, last_x = gx == 0, gx == nx - 1
    first_y, last_y = gy == 0, gy == ny - 1

    barrier = pltpu.get_barrier_semaphore()
    for d in COARSE:
        pl.semaphore_signal(barrier, inc=1, device_id=at(*d), device_id_type=MESH)

    loads = [pltpu.make_async_copy(w1, w1_v, local_sems.at[0])]
    loads += [pltpu.make_async_copy(image.at[:, r], x_v.at[r + 1], local_sems.at[r + 1]) for r in range(4)]
    loads += [pltpu.make_async_copy(src, dst, local_sems.at[5 + i]) for i, (src, dst) in enumerate(
        ((w2, w2_v), (w3, w3_v), (b1, b1_s), (b2, b2_s), (b3, b3_s)))]
    for load in loads:
        load.start()

    loads[0].wait()
    q1 = onehot(iota((32, 512), 1) // 16 == iota((32, 512), 0))
    u1[...] = mm(w1_v[...].reshape(864, 32), q1).reshape(27, 32, 512)
    build_banded(u1, t1, 32, 512, 16, 2, 2)

    for load in loads[1:5]:
        load.wait()
    ends = jnp.zeros((16, 512), F32)
    r16, l16 = iota((16, 256), 0), iota((16, 256), 1)
    for r in range(4):
        pick = onehot(((r16 == 2 * r) & (l16 == 0)) | ((r16 == 2 * r + 1) & (l16 == 255)))
        ends = ends + mm_nt(pick, x_v[r + 1].reshape(512, 256))
    own_pk[...] = ends.astype(BF)

    pl.semaphore_wait(barrier, len(COARSE))

    fine = {}
    for i, d in enumerate(FINE):
        back = FINE.index((-d[0], -d[1]))
        fine[d] = pltpu.make_async_remote_copy(
            src_ref=own_pk, dst_ref=fine_pk.at[back], send_sem=send_f.at[i], recv_sem=recv_f.at[back],
            device_id=at(*d), device_id_type=MESH)
        fine[d].start()

    def row_copy(i, h):
        r, dst, dx = ((0, 5, -1), (3, 0, 1))[i]
        chans = pl.ds(h * 16, 16)
        return pltpu.make_async_remote_copy(
            src_ref=image.at[chans, r], dst_ref=x_v.at[dst, chans], send_sem=send_x.at[i, h],
            recv_sem=recv_x.at[i, h], device_id=at(dx, 0), device_id_type=MESH)

    for h in range(2):
        for i in range(2):
            row_copy(i, h).start()

    for load in loads[5:]:
        load.wait()
    for src, dst, n in ((b1_s, bias1, 32), (b2_s, bias2, 64), (b3_s, bias3, 64)):
        for o in range(n):
            dst[o * 8:(o + 1) * 8, :] = jnp.full((8, 128), src[o], F32)

    q2 = onehot(iota((32, 256), 1) // 8 == iota((32, 256), 0))
    for tap in range(27):
        u2[tap] = mm_tn(w2_v[tap], q2)
    build_banded(u2, t2, 64, 256, 8, 1, 1)

    q3 = onehot(iota((64, 512), 1) // 8 == iota((64, 512), 0))
    u3[...] = mm(w3_v[...].reshape(1728, 64), q3).reshape(27, 64, 512)
    build_banded(u3, t3, 64, 512, 8, 1, 1)

    sy, sl = iota((256, 512), 0), iota((256, 512), 1)
    split[...] = onehot(sy == 2 * (sl % 128) + sl // 128 - 1)
    ys, js = iota((128, 256), 0), iota((128, 256), 1)
    shift[...] = onehot(ys == jnp.where(js < 128, js - 1, js - 127))

    def stack(i, h, pack, left, right, keep):
        d = mm(x_v[i, pl.ds(h * 16, 16)].reshape(256, 256), split[...])
        r32, l32 = iota((32, 256), 0), iota((32, 256), 1)
        pick = onehot(((r32 == left) & (l32 == 0)) | ((r32 == right) & (l32 == 255)))
        e = mm_tn(pack, pick)
        full = jnp.concatenate([d[:, :128] + e[:, :128], d[:, 128:384], d[:, 384:] + e[:, 128:]], axis=1)
        if keep is not None:
            full = full * keep
        full = full.astype(BF)
        for f in range(3):
            start = pl.multiple_of(i * 1536 + h * 768 + f * 256, 256)
            bb[pl.ds(start, 256), :] = full[:, f * 128:f * 128 + 256]

    fine[(0, 1)].wait_recv()
    fine[(0, -1)].wait_recv()

    def own_row(i, carry):
        left = jnp.where(first_y, -1, 2 * (i - 1) + 1)
        right = jnp.where(last_y, -1, 16 + 2 * (i - 1))
        for h in range(2):
            stack(i, h, fine_pk[0:2, :, h * 256:(h + 1) * 256].reshape(32, 256), left, right, None)
        return carry

    lax.fori_loop(1, 5, own_row, 0)

    acc[0] = mm(t1[:, 1536:], bb[1536:4608, :])
    acc[3] = mm(t1[:, :3072], bb[4608:7680, :])

    def middle(i, carry):
        acc[i] = mm(t1[...], bb[pl.ds(pl.multiple_of(i * 1536, 512), 4608), :])
        return carry

    lax.fori_loop(1, 3, middle, 0)

    r144 = iota((144, 256), 0)
    l144 = iota((144, 256), 1)
    for jj in range(6):
        dx, j = ((-1, 0, 1)[jj // 2], jj % 2)
        left = slot_of(dx, -1) * 16 + j * 4 + 3
        right = slot_of(dx, 1) * 16 + j * 4
        sel[:, jj * 256:(jj + 1) * 256] = onehot(
            ((r144 == left) & (l144 == 0)) | ((r144 == right) & (l144 == 255)))
    re, le = iota((144, 128), 0), iota((144, 128), 1)
    xo, side = le // 2, le % 2
    for a in range(3):
        jj = xo + a
        group = jnp.where(jj < 2, 1, jnp.where(jj < 4, 0, 2))
        for f in range(3):
            dyl, cil = ((1, 2), (1, 3), (0, 0))[f]
            dyr, cir = ((0, 3), (2, 0), (2, 1))[f]
            want = jnp.where(side == 0, dyl * 16 + cil, dyr * 16 + cir) + group * 48 + (jj % 2) * 4
            tile = 1536 + (a * 3 + f) * 128
            sel[:, tile:tile + 128] = onehot((re == want) & (le < 8))

    for d in FINE[2:]:
        fine[d].wait_recv()

    def halo_half(h, carry):
        for i, row, base, r, edge in ((1, 0, 2, 3, first_x), (0, 5, 4, 0, last_x)):
            row_copy(i, h).wait_recv()
            left = jnp.where(first_y, -1, 2 * r + 1)
            right = jnp.where(last_y, -1, 16 + 2 * r)
            pack = fine_pk[base:base + 2, :, pl.ds(pl.multiple_of(h * 256, 256), 256)].reshape(32, 256)
            stack(row, h, pack, left, right, jnp.where(edge, 0.0, 1.0))
        k = pl.multiple_of(h * 768, 256)
        acc[0] += mm(t1[:, pl.ds(k, 768)], bb[pl.ds(k, 768), :])
        acc[3] += mm(t1[:, pl.ds(3072 + k, 768)], bb[pl.ds(7680 + k, 768), :])
        return carry

    lax.fori_loop(0, 2, halo_half, 0)

    def pooled_copy(i, j):
        dst, dx = ((p_right, -1), (p_left, 1))[i]
        return pltpu.make_async_remote_copy(
            src_ref=p_own.at[j], dst_ref=dst.at[j], send_sem=send_p.at[i, j], recv_sem=recv_p.at[i, j],
            device_id=at(dx, 0), device_id_type=MESH)

    for j in range(2):
        m = jnp.maximum(acc[2 * j], acc[2 * j + 1])
        m = jnp.maximum(m[:, :128], m[:, 128:])
        m = jnp.maximum(m[:256], m[256:])
        p_own[j] = jnp.maximum(m + bias1[...], 0.0).astype(BF)
        for i in range(2):
            pooled_copy(i, j).start()

    ends = jnp.zeros((16, 256), F32)
    r16, l16 = iota((16, 128), 0), iota((16, 128), 1)
    for j in range(2):
        pick = onehot((r16 // 4 == j) & (l16 == jnp.where(r16 % 4 < 2, r16 % 4, 124 + r16 % 4)))
        ends = ends + mm_nt(pick, p_own[j])
    own_pk2[...] = ends.astype(BF)
    coarse = {}
    for i, d in enumerate(COARSE):
        back = COARSE.index((-d[0], -d[1]))
        coarse[d] = pltpu.make_async_remote_copy(
            src_ref=own_pk2, dst_ref=coarse_pk.at[slot_of(-d[0], -d[1])], send_sem=send_c.at[i],
            recv_sem=recv_c.at[back], device_id=at(*d), device_id_type=MESH)
        coarse[d].start()
    coarse_pk[0] = ends.astype(BF)

    def known(packs, n):
        rr = iota((n, 256), 0) // 16
        gone_x = ((rr // 3 == 1) & first_x) | ((rr // 3 == 2) & last_x)
        gone_y = ((rr % 3 == 1) & first_y) | ((rr % 3 == 2) & last_y)
        return jnp.where(gone_x | gone_y, 0.0, packs.astype(F32)).astype(BF)

    def place(p, ends, spots):
        g = (mm(p, shift[...]) + ends).astype(BF)
        parts = (g[:, :128], p, g[:, 128:])
        for ref, half in spots:
            for f in range(3):
                ref[f * 256:(f + 1) * 256, half * 128:(half + 1) * 128] = parts[f]

    coarse[(0, 1)].wait_recv()
    coarse[(0, -1)].wait_recv()
    e = mm_tn(known(coarse_pk[0:3].reshape(48, 256), 48), sel[0:48, 512:1024])
    place(p_own[0], e[:, :256], ((p_mid, 0),))
    place(p_own[1], e[:, 256:], ((p_mid, 1),))

    def own_second(m, carry):
        rows = pl.ds(pl.multiple_of(m * 256, 256), 256)
        parts = [mm(t2[rows, a * 768:(a + 1) * 768], p_mid[...]) for a in range(3)]
        s_acc[rows, 0:128] = parts[2][:, :128]
        s_acc[rows, 128:256] = parts[2][:, 128:] + parts[1][:, :128]
        s_acc[rows, 256:384] = parts[1][:, 128:] + parts[0][:, :128]
        s_acc[rows, 384:512] = parts[0][:, 128:]
        return carry

    lax.fori_loop(0, 2, own_second, 0)

    for d in COARSE[2:]:
        coarse[d].wait_recv()
    e = mm_tn(known(coarse_pk[...].reshape(144, 256), 144), sel[...])
    for k in range(9):
        p_edge[k * 256:(k + 1) * 256, :] = e[:, 1536 + k * 128:1664 + k * 128].astype(BF)
    lane = iota((1, 640), 1)
    tile, low = lane // 128, lane % 128
    row = jnp.where(tile < 4, tile, low // 2)
    gone = ((row == 0) & first_x) | ((row == 3) & last_x)
    gone = gone | ((tile == 4) & (((low % 2 == 0) & first_y) | ((low % 2 == 1) & last_y)))
    keep = jnp.where(gone, 0.0, 1.0)

    def edges(m, carry):
        rows = pl.ds(pl.multiple_of(m * 256, 256), 256)
        total = mm(t2[rows, :], p_edge[...]) + bias2[rows, :]
        s_v[rows, 512:640] = (jnp.maximum(total, 0.0) * keep[:, 512:640]).astype(BF)
        return carry

    lax.fori_loop(0, 2, edges, 0)

    for j in range(2):
        for i, src, base, edge in ((1, p_left, 0, first_x), (0, p_right, 4, last_x)):
            pooled_copy(i, j).wait_recv()
            jj = base + j
            spots = {0: ((p_lo, 0),), 1: ((p_lo, 1), (p_mix, 0)), 4: ((p_mix, 1), (p_hi, 0)), 5: ((p_hi, 1),)}[jj]
            p = (src[j].astype(F32) * jnp.where(edge, 0.0, 1.0)).astype(BF)
            place(p, e[:, jj * 256:(jj + 1) * 256], spots)

    def second(m, carry):
        rows = pl.ds(pl.multiple_of(m * 256, 256), 256)
        lo = mm(t2[rows, 0:768], p_lo[...])
        mix = mm(t2[rows, 768:1536], p_mix[...])
        hi = mm(t2[rows, 1536:2304], p_hi[...])
        added = (lo[:, :128] + mix[:, :128], lo[:, 128:], hi[:, :128], mix[:, 128:] + hi[:, 128:])
        for t in range(4):
            cut = slice(t * 128, (t + 1) * 128)
            total = s_acc[rows, cut] + added[t]
            s_v[rows, cut] = (jnp.maximum(total + bias2[rows, :], 0.0) * keep[:, cut]).astype(BF)
        return carry

    lax.fori_loop(0, 2, second, 0)

    ye, je = iota((128, 256), 0), iota((128, 256), 1)
    for x in range(4):
        mid = s_v[:, x * 128:(x + 1) * 128]
        pick = onehot(((ye == 2 * x) & (je == 0)) | ((ye == 2 * x + 1) & (je == 255)))
        both = jnp.concatenate([mid, s_v[:, 512:640]], axis=1)
        g = mm(both, jnp.concatenate([shift[...], pick], axis=0)).astype(BF)
        parts = (g[:, :128], mid, g[:, 128:])
        for a in range(3):
            if 0 <= x - a < 2:
                for f in range(3):
                    top = (a * 3 + f) * 512
                    s3[top:top + 512, (x - a) * 128:(x - a + 1) * 128] = parts[f]

    def third(m, carry):
        rows = pl.ds(pl.multiple_of(m * 256, 256), 256)
        c = mm(t3[rows, :], s3[...])
        for x in range(2):
            block = jnp.maximum(c[:, x * 128:(x + 1) * 128] + bias3[rows, :], 0.0)
            out[pl.ds(m * 32, 32), x] = block.reshape(32, 8, 128).astype(BF)
        return carry

    lax.fori_loop(0, 2, third, 0)

    for i in range(2):
        for h in range(2):
            row_copy(i, h).wait_send()
            pooled_copy(i, h).wait_send()
    for copy in list(fine.values()) + list(coarse.values()):
        copy.wait_send()


def per_device(image, w_first, b_first, w_second, b_second, w_third, b_third):
    nx, ny = lax.axis_size("gx"), lax.axis_size("gy")
    w1 = jnp.transpose(w_first, (2, 3, 4, 0, 1)).reshape(27, 32, 32)
    w2 = jnp.transpose(w_second, (2, 3, 4, 1, 0)).reshape(27, 32, 64)
    w3 = jnp.transpose(w_third, (2, 3, 4, 0, 1)).reshape(27, 64, 64)
    anywhere = pl.BlockSpec(memory_space=pltpu.HBM)
    dma = pltpu.SemaphoreType.DMA
    return pl.pallas_call(
        functools.partial(kernel, nx, ny),
        out_shape=jax.ShapeDtypeStruct((64, 2, 8, 128), BF),
        in_specs=[anywhere] * 7,
        out_specs=pl.BlockSpec(memory_space=pltpu.VMEM),
        scratch_shapes=[
            pltpu.VMEM((6, 32, 16, 256), BF),
            pltpu.VMEM((27, 32, 32), BF),
            pltpu.VMEM((27, 32, 64), BF),
            pltpu.VMEM((27, 64, 64), BF),
            pltpu.VMEM((27, 32, 512), F32),
            pltpu.VMEM((27, 64, 256), F32),
            pltpu.VMEM((27, 64, 512), F32),
            pltpu.VMEM((512, 4608), BF),
            pltpu.VMEM((512, 2304), BF),
            pltpu.VMEM((512, 4608), BF),
            pltpu.VMEM((9216, 256), BF),
            pltpu.VMEM((4, 512, 256), F32),
            pltpu.VMEM((256, 512), BF),
            pltpu.VMEM((128, 256), BF),
            pltpu.VMEM((6, 16, 512), BF),
            pltpu.VMEM((16, 512), BF),
            pltpu.VMEM((144, 2688), BF),
            pltpu.VMEM((2, 256, 128), BF),
            pltpu.VMEM((2, 256, 128), BF),
            pltpu.VMEM((2, 256, 128), BF),
            pltpu.VMEM((9, 16, 256), BF),
            pltpu.VMEM((16, 256), BF),
            pltpu.VMEM((768, 256), BF),
            pltpu.VMEM((768, 256), BF),
            pltpu.VMEM((768, 256), BF),
            pltpu.VMEM((768, 256), BF),
            pltpu.VMEM((2304, 128), BF),
            pltpu.VMEM((512, 512), F32),
            pltpu.VMEM((512, 640), BF),
            pltpu.VMEM((4608, 256), BF),
            pltpu.VMEM((256, 128), F32),
            pltpu.VMEM((512, 128), F32),
            pltpu.VMEM((512, 128), F32),
            pltpu.SMEM((32,), F32),
            pltpu.SMEM((64,), F32),
            pltpu.SMEM((64,), F32),
            dma((10,)), dma((2, 2)), dma((2, 2)), dma((6,)), dma((6,)),
            dma((2, 2)), dma((2, 2)), dma((8,)), dma((8,)),
        ],
        compiler_params=pltpu.CompilerParams(
            collective_id=0, has_side_effects=True, vmem_limit_bytes=48 * 1024 * 1024),
        name="encoder",
    )(*(pltpu.with_memory_space_constraint(v, pltpu.HBM)
        for v in (image, w1, b_first, w2, b_second, w3, b_third)))


def solution(mesh):
    placed = (P(None, "gx", None, "gy"), P(), P(), P(), P(), P(), P())
    return jax.shard_map(
        per_device, mesh=mesh, in_specs=placed, out_specs=P(None, "gx", None, "gy"), check_vma=False
    )
```

```python
import functools

import jax
import jax.numpy as jnp
from jax import lax
from jax.experimental import pallas as pl
from jax.experimental.pallas import tpu as pltpu
from jax.sharding import PartitionSpec as P

BF = jnp.bfloat16
F32 = jnp.float32
MESH = pl.DeviceIdType.MESH

FINE = ((0, -1), (0, 1), (-1, -1), (-1, 1), (1, -1), (1, 1))
COARSE = ((0, -1), (0, 1), (-1, 0), (-1, -1), (-1, 1), (1, 0), (1, -1), (1, 1))


def slot_of(dx, dy):
    order = {0: 0, -1: 1, 1: 2}
    return 3 * order[dx] + order[dy]


def iota(shape, dim):
    return lax.broadcasted_iota(jnp.int32, shape, dim)


def onehot(cond):
    return jnp.where(cond, 1.0, 0.0).astype(BF)


def mm(a, b):
    return jnp.dot(a, b, preferred_element_type=F32)


def mm_tn(a, b):
    return lax.dot_general(a, b, (((0,), (0,)), ((), ())), preferred_element_type=F32)


def mm_nt(a, b):
    return lax.dot_general(a, b, (((1,), (1,)), ((), ())), preferred_element_type=F32)


def build_banded(u_ref, t_ref, chans, lanes, depth, parities, groups):
    row = iota((8, 128), 0)
    z_in = iota((8, 128), 1) % depth

    def tap(k, carry):
        a, f = k // 3, k % 3
        for par in range(parities):
            masks = [z_in == parities * row + par + e - 1 for e in range(3)]
            for pair in range(chans // 2):
                for lt in range(lanes // 128):
                    halves = []
                    for o in (2 * pair, 2 * pair + 1):
                        value = jnp.zeros((8, 128), F32)
                        for e in range(3):
                            line = u_ref[(a * 3 + e) * 3 + f, o:o + 1, lt * 128:(lt + 1) * 128]
                            value = jnp.where(masks[e], jnp.broadcast_to(line, (8, 128)), value)
                        halves.append(value)
                    block = jnp.concatenate(halves, axis=0).astype(BF)
                    top = par * chans * 8 + pair * 16
                    part = lanes // groups
                    group, rest = lt * 128 // part, lt * 128 % part
                    lane = a * (3 * lanes) + f * part + (group * 3 * part + rest)
                    t_ref[top:top + 16, pl.ds(pl.multiple_of(lane, 128), 128)] = block
        return carry

    lax.fori_loop(0, 9, tap, 0)


def kernel(nx, ny, image, w1, b1, w2, b2, w3, b3, out,
           x_v, w1_v, w2_v, w3_v, u1, u2, u3, t1, t2, t3, bb, acc, split, shift, fine_pk, own_pk,
           sel, p_own, p_left, p_right, coarse_pk, own_pk2, p_mid, p_lo, p_hi, p_mix, p_edge, s_acc, s_v, s3,
           bias1, bias2, bias3, b1_s, b2_s, b3_s,
           local_sems, send_x, recv_x, send_f, recv_f, send_p, recv_p, send_c, recv_c):
    gx, gy = lax.axis_index("gx"), lax.axis_index("gy")

    def at(dx, dy):
        return (lax.rem(gx + dx + nx, nx), lax.rem(gy + dy + ny, ny))

    first_x, last_x = gx == 0, gx == nx - 1
    first_y, last_y = gy == 0, gy == ny - 1

    barrier = pltpu.get_barrier_semaphore()
    for d in COARSE:
        pl.semaphore_signal(barrier, inc=1, device_id=at(*d), device_id_type=MESH)

    loads = [pltpu.make_async_copy(w1, w1_v, local_sems.at[0])]
    loads += [pltpu.make_async_copy(image.at[:, r], x_v.at[r + 1], local_sems.at[r + 1]) for r in range(4)]
    loads += [pltpu.make_async_copy(src, dst, local_sems.at[5 + i]) for i, (src, dst) in enumerate(
        ((w2, w2_v), (w3, w3_v), (b1, b1_s), (b2, b2_s), (b3, b3_s)))]
    for load in loads:
        load.start()

    loads[0].wait()
    q1 = onehot(iota((32, 512), 1) // 16 == iota((32, 512), 0))
    u1[...] = mm(w1_v[...].reshape(864, 32), q1).reshape(27, 32, 512)
    build_banded(u1, t1, 32, 512, 16, 2, 2)

    for load in loads[1:5]:
        load.wait()
    ends = jnp.zeros((8, 512), F32)
    r16, l16 = iota((8, 256), 0), iota((8, 256), 1)
    for r in range(4):
        pick = onehot(((r16 == 2 * r) & (l16 == 0)) | ((r16 == 2 * r + 1) & (l16 == 255)))
        ends = ends + mm_nt(pick, x_v[r + 1].reshape(512, 256))
    own_pk[...] = ends.astype(BF)

    pl.semaphore_wait(barrier, len(COARSE))

    fine = {}
    for i, d in enumerate(FINE):
        back = FINE.index((-d[0], -d[1]))
        fine[d] = pltpu.make_async_remote_copy(
            src_ref=own_pk, dst_ref=fine_pk.at[back], send_sem=send_f.at[i], recv_sem=recv_f.at[back],
            device_id=at(*d), device_id_type=MESH)
        fine[d].start()

    def row_copy(i, h):
        r, dst, dx = ((0, 5, -1), (3, 0, 1))[i]
        chans = pl.ds(h * 16, 16)
        return pltpu.make_async_remote_copy(
            src_ref=image.at[chans, r], dst_ref=x_v.at[dst, chans], send_sem=send_x.at[i, h],
            recv_sem=recv_x.at[i, h], device_id=at(dx, 0), device_id_type=MESH)

    for h in range(2):
        for i in range(2):
            row_copy(i, h).start()

    for load in loads[5:]:
        load.wait()
    for src, dst, n in ((b1_s, bias1, 32), (b2_s, bias2, 64), (b3_s, bias3, 64)):
        for o in range(n):
            dst[o * 8:(o + 1) * 8, :] = jnp.full((8, 128), src[o], F32)

    q2 = onehot(iota((32, 256), 1) // 8 == iota((32, 256), 0))
    for tap in range(27):
        u2[tap] = mm_tn(w2_v[tap], q2)
    build_banded(u2, t2, 64, 256, 8, 1, 1)

    q3 = onehot(iota((64, 512), 1) // 8 == iota((64, 512), 0))
    u3[...] = mm(w3_v[...].reshape(1728, 64), q3).reshape(27, 64, 512)
    build_banded(u3, t3, 64, 512, 8, 1, 1)

    sy, sl = iota((256, 512), 0), iota((256, 512), 1)
    split[...] = onehot(sy == 2 * (sl % 128) + sl // 128 - 1)
    ys, js = iota((128, 256), 0), iota((128, 256), 1)
    shift[...] = onehot(ys == jnp.where(js < 128, js - 1, js - 127))

    def stack(i, h, pack, left, right, keep):
        d = mm(x_v[i, pl.ds(h * 16, 16)].reshape(256, 256), split[...])
        r32, l32 = iota((16, 256), 0), iota((16, 256), 1)
        pick = onehot(((r32 == left) & (l32 == 0)) | ((r32 == right) & (l32 == 255)))
        e = mm_tn(pack.astype(F32).reshape(16, 256).astype(BF), pick)
        full = jnp.concatenate([d[:, :128] + e[:, :128], d[:, 128:384], d[:, 384:] + e[:, 128:]], axis=1)
        if keep is not None:
            full = full * keep
        full = full.astype(BF)
        for f in range(3):
            start = pl.multiple_of(i * 1536 + h * 768 + f * 256, 256)
            bb[pl.ds(start, 256), :] = full[:, f * 128:f * 128 + 256]

    fine[(0, 1)].wait_recv()
    fine[(0, -1)].wait_recv()

    def own_row(i, carry):
        left = jnp.where(first_y, -1, 2 * (i - 1) + 1)
        right = jnp.where(last_y, -1, 8 + 2 * (i - 1))
        for h in range(2):
            stack(i, h, fine_pk[0:2, :, h * 256:(h + 1) * 256], left, right, None)
        return carry

    lax.fori_loop(1, 5, own_row, 0)

    acc[0] = mm(t1[:, 1536:], bb[1536:4608, :])
    acc[3] = mm(t1[:, :3072], bb[4608:7680, :])

    def middle(i, carry):
        acc[i] = mm(t1[...], bb[pl.ds(pl.multiple_of(i * 1536, 512), 4608), :])
        return carry

    lax.fori_loop(1, 3, middle, 0)

    r144 = iota((72, 256), 0)
    l144 = iota((72, 256), 1)
    for jj in range(6):
        dx, j = ((-1, 0, 1)[jj // 2], jj % 2)
        left = slot_of(dx, -1) * 8 + j * 4 + 3
        right = slot_of(dx, 1) * 8 + j * 4
        sel[:, jj * 256:(jj + 1) * 256] = onehot(
            ((r144 == left) & (l144 == 0)) | ((r144 == right) & (l144 == 255)))
    re, le = iota((72, 128), 0), iota((72, 128), 1)
    xo, side = le // 2, le % 2
    for a in range(3):
        jj = xo + a
        group = jnp.where(jj < 2, 1, jnp.where(jj < 4, 0, 2))
        for f in range(3):
            dyl, cil = ((1, 2), (1, 3), (0, 0))[f]
            dyr, cir = ((0, 3), (2, 0), (2, 1))[f]
            want = jnp.where(side == 0, dyl * 8 + cil, dyr * 8 + cir) + group * 24 + (jj % 2) * 4
            tile = 1536 + (a * 3 + f) * 128
            sel[:, tile:tile + 128] = onehot((re == want) & (le < 8))

    for d in FINE[2:]:
        fine[d].wait_recv()

    def halo_half(h, carry):
        for i, row, base, r, edge in ((1, 0, 2, 3, first_x), (0, 5, 4, 0, last_x)):
            row_copy(i, h).wait_recv()
            left = jnp.where(first_y, -1, 2 * r + 1)
            right = jnp.where(last_y, -1, 8 + 2 * r)
            pack = fine_pk[base:base + 2, :, pl.ds(pl.multiple_of(h * 256, 256), 256)]
            stack(row, h, pack, left, right, jnp.where(edge, 0.0, 1.0))
        k = pl.multiple_of(h * 768, 256)
        acc[0] += mm(t1[:, pl.ds(k, 768)], bb[pl.ds(k, 768), :])
        acc[3] += mm(t1[:, pl.ds(3072 + k, 768)], bb[pl.ds(7680 + k, 768), :])
        return carry

    lax.fori_loop(0, 2, halo_half, 0)

    def pooled_copy(i, j):
        dst, dx = ((p_right, -1), (p_left, 1))[i]
        return pltpu.make_async_remote_copy(
            src_ref=p_own.at[j], dst_ref=dst.at[j], send_sem=send_p.at[i, j], recv_sem=recv_p.at[i, j],
            device_id=at(dx, 0), device_id_type=MESH)

    for j in range(2):
        m = jnp.maximum(acc[2 * j], acc[2 * j + 1])
        m = jnp.maximum(m[:, :128], m[:, 128:])
        m = jnp.maximum(m[:256], m[256:])
        p_own[j] = jnp.maximum(m + bias1[...], 0.0).astype(BF)

    ends = jnp.zeros((8, 256), F32)
    r16, l16 = iota((8, 128), 0), iota((8, 128), 1)
    for j in range(2):
        pick = onehot((r16 // 4 == j) & (l16 == jnp.where(r16 % 4 < 2, r16 % 4, 124 + r16 % 4)))
        ends = ends + mm_nt(pick, p_own[j])
    own_pk2[...] = ends.astype(BF)
    coarse = {}
    for i, d in enumerate(COARSE):
        back = COARSE.index((-d[0], -d[1]))
        coarse[d] = pltpu.make_async_remote_copy(
            src_ref=own_pk2, dst_ref=coarse_pk.at[slot_of(-d[0], -d[1])], send_sem=send_c.at[i],
            recv_sem=recv_c.at[back], device_id=at(*d), device_id_type=MESH)
        coarse[d].start()
    for j in range(2):
        for i in range(2):
            pooled_copy(i, j).start()
    coarse_pk[0] = ends.astype(BF)

    def known(packs, n):
        rr = iota((n, 256), 0) // 8
        gone_x = ((rr // 3 == 1) & first_x) | ((rr // 3 == 2) & last_x)
        gone_y = ((rr % 3 == 1) & first_y) | ((rr % 3 == 2) & last_y)
        return jnp.where(gone_x | gone_y, 0.0, packs.astype(F32).reshape(n, 256)).astype(BF)

    def place(p, ends, spots):
        g = (mm(p, shift[...]) + ends).astype(BF)
        parts = (g[:, :128], p, g[:, 128:])
        for ref, half in spots:
            for f in range(3):
                ref[f * 256:(f + 1) * 256, half * 128:(half + 1) * 128] = parts[f]

    coarse[(0, 1)].wait_recv()
    coarse[(0, -1)].wait_recv()
    e = mm_tn(known(coarse_pk[0:3], 24), sel[0:24, 512:1024])
    place(p_own[0], e[:, :256], ((p_mid, 0),))
    place(p_own[1], e[:, 256:], ((p_mid, 1),))

    def own_second(m, carry):
        rows = pl.ds(pl.multiple_of(m * 256, 256), 256)
        parts = [mm(t2[rows, a * 768:(a + 1) * 768], p_mid[...]) for a in range(3)]
        s_acc[rows, 0:128] = parts[2][:, :128]
        s_acc[rows, 128:256] = parts[2][:, 128:] + parts[1][:, :128]
        s_acc[rows, 256:384] = parts[1][:, 128:] + parts[0][:, :128]
        s_acc[rows, 384:512] = parts[0][:, 128:]
        return carry

    lax.fori_loop(0, 2, own_second, 0)

    for d in COARSE[2:]:
        coarse[d].wait_recv()
    e = mm_tn(known(coarse_pk[...], 72), sel[...])
    for k in range(9):
        p_edge[k * 256:(k + 1) * 256, :] = e[:, 1536 + k * 128:1664 + k * 128].astype(BF)
    lane = iota((1, 640), 1)
    tile, low = lane // 128, lane % 128
    row = jnp.where(tile < 4, tile, low // 2)
    gone = ((row == 0) & first_x) | ((row == 3) & last_x)
    gone = gone | ((tile == 4) & (((low % 2 == 0) & first_y) | ((low % 2 == 1) & last_y)))
    keep = jnp.where(gone, 0.0, 1.0)

    def edges(m, carry):
        rows = pl.ds(pl.multiple_of(m * 256, 256), 256)
        total = mm(t2[rows, :], p_edge[...]) + bias2[rows, :]
        s_v[rows, 512:640] = (jnp.maximum(total, 0.0) * keep[:, 512:640]).astype(BF)
        return carry

    lax.fori_loop(0, 2, edges, 0)

    for j in range(2):
        for i, src, base, edge in ((1, p_left, 0, first_x), (0, p_right, 4, last_x)):
            pooled_copy(i, j).wait_recv()
            jj = base + j
            spots = {0: ((p_lo, 0),), 1: ((p_lo, 1), (p_mix, 0)), 4: ((p_mix, 1), (p_hi, 0)), 5: ((p_hi, 1),)}[jj]
            p = (src[j].astype(F32) * jnp.where(edge, 0.0, 1.0)).astype(BF)
            place(p, e[:, jj * 256:(jj + 1) * 256], spots)

    def second(m, carry):
        rows = pl.ds(pl.multiple_of(m * 256, 256), 256)
        lo = mm(t2[rows, 0:768], p_lo[...])
        mix = mm(t2[rows, 768:1536], p_mix[...])
        hi = mm(t2[rows, 1536:2304], p_hi[...])
        added = (lo[:, :128] + mix[:, :128], lo[:, 128:], hi[:, :128], mix[:, 128:] + hi[:, 128:])
        for t in range(4):
            cut = slice(t * 128, (t + 1) * 128)
            total = s_acc[rows, cut] + added[t]
            s_v[rows, cut] = (jnp.maximum(total + bias2[rows, :], 0.0) * keep[:, cut]).astype(BF)
        return carry

    lax.fori_loop(0, 2, second, 0)

    ye, je = iota((128, 256), 0), iota((128, 256), 1)
    for x in range(4):
        mid = s_v[:, x * 128:(x + 1) * 128]
        pick = onehot(((ye == 2 * x) & (je == 0)) | ((ye == 2 * x + 1) & (je == 255)))
        both = jnp.concatenate([mid, s_v[:, 512:640]], axis=1)
        g = mm(both, jnp.concatenate([shift[...], pick], axis=0)).astype(BF)
        parts = (g[:, :128], mid, g[:, 128:])
        for a in range(3):
            if 0 <= x - a < 2:
                for f in range(3):
                    top = (a * 3 + f) * 512
                    s3[top:top + 512, (x - a) * 128:(x - a + 1) * 128] = parts[f]

    def third(m, carry):
        rows = pl.ds(pl.multiple_of(m * 256, 256), 256)
        c = mm(t3[rows, :], s3[...])
        for x in range(2):
            block = jnp.maximum(c[:, x * 128:(x + 1) * 128] + bias3[rows, :], 0.0)
            out[pl.ds(m * 32, 32), x] = block.reshape(32, 8, 128).astype(BF)
        return carry

    lax.fori_loop(0, 2, third, 0)

    for i in range(2):
        for h in range(2):
            row_copy(i, h).wait_send()
            pooled_copy(i, h).wait_send()
    for copy in list(fine.values()) + list(coarse.values()):
        copy.wait_send()


def per_device(image, w_first, b_first, w_second, b_second, w_third, b_third):
    nx, ny = lax.axis_size("gx"), lax.axis_size("gy")
    w1 = jnp.transpose(w_first, (2, 3, 4, 0, 1)).reshape(27, 32, 32)
    w2 = jnp.transpose(w_second, (2, 3, 4, 1, 0)).reshape(27, 32, 64)
    w3 = jnp.transpose(w_third, (2, 3, 4, 0, 1)).reshape(27, 64, 64)
    anywhere = pl.BlockSpec(memory_space=pltpu.HBM)
    dma = pltpu.SemaphoreType.DMA
    return pl.pallas_call(
        functools.partial(kernel, nx, ny),
        out_shape=jax.ShapeDtypeStruct((64, 2, 8, 128), BF),
        in_specs=[anywhere] * 7,
        out_specs=pl.BlockSpec(memory_space=pltpu.VMEM),
        scratch_shapes=[
            pltpu.VMEM((6, 32, 16, 256), BF),
            pltpu.VMEM((27, 32, 32), BF),
            pltpu.VMEM((27, 32, 64), BF),
            pltpu.VMEM((27, 64, 64), BF),
            pltpu.VMEM((27, 32, 512), F32),
            pltpu.VMEM((27, 64, 256), F32),
            pltpu.VMEM((27, 64, 512), F32),
            pltpu.VMEM((512, 4608), BF),
            pltpu.VMEM((512, 2304), BF),
            pltpu.VMEM((512, 4608), BF),
            pltpu.VMEM((9216, 256), BF),
            pltpu.VMEM((4, 512, 256), F32),
            pltpu.VMEM((256, 512), BF),
            pltpu.VMEM((128, 256), BF),
            pltpu.VMEM((6, 8, 512), BF),
            pltpu.VMEM((8, 512), BF),
            pltpu.VMEM((72, 2688), BF),
            pltpu.VMEM((2, 256, 128), BF),
            pltpu.VMEM((2, 256, 128), BF),
            pltpu.VMEM((2, 256, 128), BF),
            pltpu.VMEM((9, 8, 256), BF),
            pltpu.VMEM((8, 256), BF),
            pltpu.VMEM((768, 256), BF),
            pltpu.VMEM((768, 256), BF),
            pltpu.VMEM((768, 256), BF),
            pltpu.VMEM((768, 256), BF),
            pltpu.VMEM((2304, 128), BF),
            pltpu.VMEM((512, 512), F32),
            pltpu.VMEM((512, 640), BF),
            pltpu.VMEM((4608, 256), BF),
            pltpu.VMEM((256, 128), F32),
            pltpu.VMEM((512, 128), F32),
            pltpu.VMEM((512, 128), F32),
            pltpu.SMEM((32,), F32),
            pltpu.SMEM((64,), F32),
            pltpu.SMEM((64,), F32),
            dma((10,)), dma((2, 2)), dma((2, 2)), dma((6,)), dma((6,)),
            dma((2, 2)), dma((2, 2)), dma((8,)), dma((8,)),
        ],
        compiler_params=pltpu.CompilerParams(
            collective_id=0, has_side_effects=True, vmem_limit_bytes=48 * 1024 * 1024),
        name="encoder",
    )(*(pltpu.with_memory_space_constraint(v, pltpu.HBM)
        for v in (image, w1, b_first, w2, b_second, w3, b_third)))


def solution(mesh):
    placed = (P(None, "gx", None, "gy"), P(), P(), P(), P(), P(), P())
    return jax.shard_map(
        per_device, mesh=mesh, in_specs=placed, out_specs=P(None, "gx", None, "gy"), check_vma=False
    )
```

```python
import functools

import jax
import jax.numpy as jnp
from jax import lax
from jax.experimental import pallas as pl
from jax.experimental.pallas import tpu as pltpu
from jax.sharding import PartitionSpec as P

BF = jnp.bfloat16
F32 = jnp.float32
MESH = pl.DeviceIdType.MESH

FINE = ((0, -1), (0, 1), (-1, -1), (-1, 1), (1, -1), (1, 1))
COARSE = ((0, -1), (0, 1), (-1, 0), (-1, -1), (-1, 1), (1, 0), (1, -1), (1, 1))


def slot_of(dx, dy):
    order = {0: 0, -1: 1, 1: 2}
    return 3 * order[dx] + order[dy]


def iota(shape, dim):
    return lax.broadcasted_iota(jnp.int32, shape, dim)


def onehot(cond):
    return jnp.where(cond, 1.0, 0.0).astype(BF)


def mm(a, b):
    return jnp.dot(a, b, preferred_element_type=F32)


def mm_tn(a, b):
    return lax.dot_general(a, b, (((0,), (0,)), ((), ())), preferred_element_type=F32)


def mm_nt(a, b):
    return lax.dot_general(a, b, (((1,), (1,)), ((), ())), preferred_element_type=F32)


def build_banded(u_ref, t_ref, chans, lanes, depth, parities, groups):
    row = iota((8, 128), 0)
    z_in = iota((8, 128), 1) % depth

    def tap(k, carry):
        a, f = k // 3, k % 3
        for par in range(parities):
            masks = [z_in == parities * row + par + e - 1 for e in range(3)]
            for pair in range(chans // 2):
                for lt in range(lanes // 128):
                    halves = []
                    for o in (2 * pair, 2 * pair + 1):
                        value = jnp.zeros((8, 128), F32)
                        for e in range(3):
                            line = u_ref[(a * 3 + e) * 3 + f, o:o + 1, lt * 128:(lt + 1) * 128]
                            value = jnp.where(masks[e], jnp.broadcast_to(line, (8, 128)), value)
                        halves.append(value)
                    block = jnp.concatenate(halves, axis=0).astype(BF)
                    top = par * chans * 8 + pair * 16
                    part = lanes // groups
                    group, rest = lt * 128 // part, lt * 128 % part
                    lane = a * (3 * lanes) + f * part + (group * 3 * part + rest)
                    t_ref[top:top + 16, pl.ds(pl.multiple_of(lane, 128), 128)] = block
        return carry

    lax.fori_loop(0, 9, tap, 0)


def kernel(nx, ny, image, w1, b1, w2, b2, w3, b3, out,
           x_v, w1_v, w2_v, w3_v, u1, u2, u3, t1, t2, t3, bb, acc, split, shift, fine_pk, own_pk,
           sel, p_own, p_left, p_right, coarse_pk, own_pk2, p_mid, p_lo, p_hi, p_mix, p_edge, s_acc, s_v, s3,
           bias1, bias2, bias3, b1_s, b2_s, b3_s,
           local_sems, send_x, recv_x, send_f, recv_f, send_p, recv_p, send_c, recv_c):
    gx, gy = lax.axis_index("gx"), lax.axis_index("gy")

    def at(dx, dy):
        return (lax.rem(gx + dx + nx, nx), lax.rem(gy + dy + ny, ny))

    first_x, last_x = gx == 0, gx == nx - 1
    first_y, last_y = gy == 0, gy == ny - 1

    barrier = pltpu.get_barrier_semaphore()
    for d in COARSE:
        pl.semaphore_signal(barrier, inc=1, device_id=at(*d), device_id_type=MESH)

    loads = [pltpu.make_async_copy(w1, w1_v, local_sems.at[0])]
    loads += [pltpu.make_async_copy(image.at[:, r], x_v.at[r + 1], local_sems.at[r + 1]) for r in range(4)]
    loads += [pltpu.make_async_copy(src, dst, local_sems.at[5 + i]) for i, (src, dst) in enumerate(
        ((w2, w2_v), (w3, w3_v), (b1, b1_s), (b2, b2_s), (b3, b3_s)))]
    for load in loads:
        load.start()

    loads[0].wait()
    q1 = onehot(iota((32, 512), 1) // 16 == iota((32, 512), 0))
    u1[...] = mm(w1_v[...].reshape(864, 32), q1).reshape(27, 32, 512)
    build_banded(u1, t1, 32, 512, 16, 2, 2)

    for load in loads[1:5]:
        load.wait()
    ends = jnp.zeros((8, 512), F32)
    r16, l16 = iota((8, 256), 0), iota((8, 256), 1)
    for r in range(4):
        pick = onehot(((r16 == 2 * r) & (l16 == 0)) | ((r16 == 2 * r + 1) & (l16 == 255)))
        ends = ends + mm_nt(pick, x_v[r + 1].reshape(512, 256))
    own_pk[...] = ends.astype(BF)

    pl.semaphore_wait(barrier, len(COARSE))

    fine = {}
    for i, d in enumerate(FINE):
        back = FINE.index((-d[0], -d[1]))
        fine[d] = pltpu.make_async_remote_copy(
            src_ref=own_pk, dst_ref=fine_pk.at[back], send_sem=send_f.at[i], recv_sem=recv_f.at[back],
            device_id=at(*d), device_id_type=MESH)
        fine[d].start()

    def row_copy(i, h):
        r, dst, dx = ((0, 5, -1), (3, 0, 1))[i]
        chans = pl.ds(h * 16, 16)
        return pltpu.make_async_remote_copy(
            src_ref=image.at[chans, r], dst_ref=x_v.at[dst, chans], send_sem=send_x.at[i, h],
            recv_sem=recv_x.at[i, h], device_id=at(dx, 0), device_id_type=MESH)

    for h in range(2):
        for i in range(2):
            row_copy(i, h).start()

    for load in loads[5:]:
        load.wait()
    for src, dst, n in ((b1_s, bias1, 32), (b2_s, bias2, 64), (b3_s, bias3, 64)):
        for o in range(n):
            dst[o * 8:(o + 1) * 8, :] = jnp.full((8, 128), src[o], F32)

    q2 = onehot(iota((32, 256), 1) // 8 == iota((32, 256), 0))
    for tap in range(27):
        u2[tap] = mm_tn(w2_v[tap], q2)
    build_banded(u2, t2, 64, 256, 8, 1, 1)

    q3 = onehot(iota((64, 512), 1) // 8 == iota((64, 512), 0))
    u3[...] = mm(w3_v[...].reshape(1728, 64), q3).reshape(27, 64, 512)
    build_banded(u3, t3, 64, 512, 8, 1, 1)

    sy, sl = iota((256, 512), 0), iota((256, 512), 1)
    split[...] = onehot(sy == 2 * (sl % 128) + sl // 128 - 1)
    ys, js = iota((128, 256), 0), iota((128, 256), 1)
    shift[...] = onehot(ys == jnp.where(js < 128, js - 1, js - 127))

    def stack(i, h, pack, left, right, keep):
        d = mm(x_v[i, pl.ds(h * 16, 16)].reshape(256, 256), split[...])
        r32, l32 = iota((16, 256), 0), iota((16, 256), 1)
        pick = onehot(((r32 == left) & (l32 == 0)) | ((r32 == right) & (l32 == 255)))
        e = mm_tn(pack.astype(F32).reshape(16, 256).astype(BF), pick)
        full = jnp.concatenate([d[:, :128] + e[:, :128], d[:, 128:384], d[:, 384:] + e[:, 128:]], axis=1)
        if keep is not None:
            full = full * keep
        full = full.astype(BF)
        for f in range(3):
            start = pl.multiple_of(i * 1536 + h * 768 + f * 256, 256)
            bb[pl.ds(start, 256), :] = full[:, f * 128:f * 128 + 256]

    fine[(0, 1)].wait_recv()
    fine[(0, -1)].wait_recv()

    def own_row(i, carry):
        left = jnp.where(first_y, -1, 2 * (i - 1) + 1)
        right = jnp.where(last_y, -1, 8 + 2 * (i - 1))
        for h in range(2):
            stack(i, h, fine_pk[0:2, :, h * 256:(h + 1) * 256], left, right, None)
        return carry

    lax.fori_loop(1, 5, own_row, 0)

    acc[0] = mm(t1[:, 1536:], bb[1536:4608, :])
    acc[3] = mm(t1[:, :3072], bb[4608:7680, :])

    def middle(i, carry):
        acc[i] = mm(t1[...], bb[pl.ds(pl.multiple_of(i * 1536, 512), 4608), :])
        return carry

    lax.fori_loop(1, 3, middle, 0)

    r144 = iota((72, 256), 0)
    l144 = iota((72, 256), 1)
    for jj in range(6):
        dx, j = ((-1, 0, 1)[jj // 2], jj % 2)
        left = slot_of(dx, -1) * 8 + j * 4 + 3
        right = slot_of(dx, 1) * 8 + j * 4
        sel[:, jj * 256:(jj + 1) * 256] = onehot(
            ((r144 == left) & (l144 == 0)) | ((r144 == right) & (l144 == 255)))
    re, le = iota((72, 128), 0), iota((72, 128), 1)
    xo, side = le // 2, le % 2
    for a in range(3):
        jj = xo + a
        group = jnp.where(jj < 2, 1, jnp.where(jj < 4, 0, 2))
        for f in range(3):
            dyl, cil = ((1, 2), (1, 3), (0, 0))[f]
            dyr, cir = ((0, 3), (2, 0), (2, 1))[f]
            want = jnp.where(side == 0, dyl * 8 + cil, dyr * 8 + cir) + group * 24 + (jj % 2) * 4
            tile = 1536 + (a * 3 + f) * 128
            sel[:, tile:tile + 128] = onehot((re == want) & (le < 8))

    for d in FINE[2:]:
        fine[d].wait_recv()

    def halo_half(h, carry):
        for i, row, base, r, edge in ((1, 0, 2, 3, first_x), (0, 5, 4, 0, last_x)):
            row_copy(i, h).wait_recv()
            left = jnp.where(first_y, -1, 2 * r + 1)
            right = jnp.where(last_y, -1, 8 + 2 * r)
            pack = fine_pk[base:base + 2, :, pl.ds(pl.multiple_of(h * 256, 256), 256)]
            stack(row, h, pack, left, right, jnp.where(edge, 0.0, 1.0))
        k = pl.multiple_of(h * 768, 256)
        acc[0] += mm(t1[:, pl.ds(k, 768)], bb[pl.ds(k, 768), :])
        acc[3] += mm(t1[:, pl.ds(3072 + k, 768)], bb[pl.ds(7680 + k, 768), :])
        return carry

    lax.fori_loop(0, 2, halo_half, 0)

    def pooled_copy(i, j):
        dst, dx = ((p_right, -1), (p_left, 1))[i]
        return pltpu.make_async_remote_copy(
            src_ref=p_own.at[j], dst_ref=dst.at[j], send_sem=send_p.at[i, j], recv_sem=recv_p.at[i, j],
            device_id=at(dx, 0), device_id_type=MESH)

    for j in range(2):
        m = jnp.maximum(acc[2 * j], acc[2 * j + 1])
        m = jnp.maximum(m[:, :128], m[:, 128:])
        m = jnp.maximum(m[:256], m[256:])
        p_own[j] = jnp.maximum(m + bias1[...], 0.0).astype(BF)

    ends = jnp.zeros((8, 256), F32)
    r16, l16 = iota((8, 128), 0), iota((8, 128), 1)
    for j in range(2):
        pick = onehot((r16 // 4 == j) & (l16 == jnp.where(r16 % 4 < 2, r16 % 4, 124 + r16 % 4)))
        ends = ends + mm_nt(pick, p_own[j])
    own_pk2[...] = ends.astype(BF)
    coarse = {}
    for i, d in enumerate(COARSE):
        back = COARSE.index((-d[0], -d[1]))
        coarse[d] = pltpu.make_async_remote_copy(
            src_ref=own_pk2, dst_ref=coarse_pk.at[slot_of(-d[0], -d[1])], send_sem=send_c.at[i],
            recv_sem=recv_c.at[back], device_id=at(*d), device_id_type=MESH)
        coarse[d].start()
    for j in range(2):
        for i in range(2):
            pooled_copy(i, j).start()
    coarse_pk[0] = ends.astype(BF)

    def known(packs, n):
        rr = iota((n, 256), 0) // 8
        gone_x = ((rr // 3 == 1) & first_x) | ((rr // 3 == 2) & last_x)
        gone_y = ((rr % 3 == 1) & first_y) | ((rr % 3 == 2) & last_y)
        return jnp.where(gone_x | gone_y, 0.0, packs.astype(F32).reshape(n, 256)).astype(BF)

    def place(p, ends, spots):
        g = (mm(p, shift[...]) + ends).astype(BF)
        parts = (g[:, :128], p, g[:, 128:])
        for ref, half in spots:
            for f in range(3):
                ref[f * 256:(f + 1) * 256, half * 128:(half + 1) * 128] = parts[f]

    coarse[(0, 1)].wait_recv()
    coarse[(0, -1)].wait_recv()
    e = mm_tn(known(coarse_pk[0:3], 24), sel[0:24, 512:1024])
    place(p_own[0], e[:, :256], ((p_mid, 0),))
    place(p_own[1], e[:, 256:], ((p_mid, 1),))

    def own_second(m, carry):
        rows = pl.ds(pl.multiple_of(m * 256, 256), 256)
        parts = [mm(t2[rows, a * 768:(a + 1) * 768], p_mid[...]) for a in range(3)]
        s_acc[rows, 0:128] = parts[2][:, :128]
        s_acc[rows, 128:256] = parts[2][:, 128:] + parts[1][:, :128]
        s_acc[rows, 256:384] = parts[1][:, 128:] + parts[0][:, :128]
        s_acc[rows, 384:512] = parts[0][:, 128:]
        return carry

    lax.fori_loop(0, 2, own_second, 0)

    for d in COARSE[2:]:
        coarse[d].wait_recv()
    packs = known(coarse_pk[...], 72)
    e = mm_tn(packs, sel[:, 1536:])
    for k in range(9):
        p_edge[k * 256:(k + 1) * 256, :] = e[:, k * 128:(k + 1) * 128].astype(BF)
    lane = iota((1, 640), 1)
    tile, low = lane // 128, lane % 128
    row = jnp.where(tile < 4, tile, low // 2)
    gone = ((row == 0) & first_x) | ((row == 3) & last_x)
    gone = gone | ((tile == 4) & (((low % 2 == 0) & first_y) | ((low % 2 == 1) & last_y)))
    keep = jnp.where(gone, 0.0, 1.0)

    def edges(m, carry):
        rows = pl.ds(pl.multiple_of(m * 256, 256), 256)
        total = mm(t2[rows, :], p_edge[...]) + bias2[rows, :]
        s_v[rows, 512:640] = (jnp.maximum(total, 0.0) * keep[:, 512:640]).astype(BF)
        return carry

    lax.fori_loop(0, 2, edges, 0)

    for j in range(2):
        for i, src, base, edge in ((1, p_left, 0, first_x), (0, p_right, 4, last_x)):
            pooled_copy(i, j).wait_recv()
            jj = base + j
            spots = {0: ((p_lo, 0),), 1: ((p_lo, 1), (p_mix, 0)), 4: ((p_mix, 1), (p_hi, 0)), 5: ((p_hi, 1),)}[jj]
            p = (src[j].astype(F32) * jnp.where(edge, 0.0, 1.0)).astype(BF)
            place(p, mm_tn(packs, sel[:, jj * 256:(jj + 1) * 256]), spots)

    def second(m, carry):
        rows = pl.ds(pl.multiple_of(m * 256, 256), 256)
        lo = mm(t2[rows, 0:768], p_lo[...])
        mix = mm(t2[rows, 768:1536], p_mix[...])
        hi = mm(t2[rows, 1536:2304], p_hi[...])
        added = (lo[:, :128] + mix[:, :128], lo[:, 128:], hi[:, :128], mix[:, 128:] + hi[:, 128:])
        for t in range(4):
            cut = slice(t * 128, (t + 1) * 128)
            total = s_acc[rows, cut] + added[t]
            s_v[rows, cut] = (jnp.maximum(total + bias2[rows, :], 0.0) * keep[:, cut]).astype(BF)
        return carry

    lax.fori_loop(0, 2, second, 0)

    ye, je = iota((128, 256), 0), iota((128, 256), 1)
    for x in range(4):
        mid = s_v[:, x * 128:(x + 1) * 128]
        pick = onehot(((ye == 2 * x) & (je == 0)) | ((ye == 2 * x + 1) & (je == 255)))
        both = jnp.concatenate([mid, s_v[:, 512:640]], axis=1)
        g = mm(both, jnp.concatenate([shift[...], pick], axis=0)).astype(BF)
        parts = (g[:, :128], mid, g[:, 128:])
        for a in range(3):
            if 0 <= x - a < 2:
                for f in range(3):
                    top = (a * 3 + f) * 512
                    s3[top:top + 512, (x - a) * 128:(x - a + 1) * 128] = parts[f]

    def third(m, carry):
        rows = pl.ds(pl.multiple_of(m * 256, 256), 256)
        c = mm(t3[rows, :], s3[...])
        for x in range(2):
            block = jnp.maximum(c[:, x * 128:(x + 1) * 128] + bias3[rows, :], 0.0)
            out[pl.ds(m * 32, 32), x] = block.reshape(32, 8, 128).astype(BF)
        return carry

    lax.fori_loop(0, 2, third, 0)

    for i in range(2):
        for h in range(2):
            row_copy(i, h).wait_send()
            pooled_copy(i, h).wait_send()
    for copy in list(fine.values()) + list(coarse.values()):
        copy.wait_send()


def per_device(image, w_first, b_first, w_second, b_second, w_third, b_third):
    nx, ny = lax.axis_size("gx"), lax.axis_size("gy")
    w1 = jnp.transpose(w_first, (2, 3, 4, 0, 1)).reshape(27, 32, 32)
    w2 = jnp.transpose(w_second, (2, 3, 4, 1, 0)).reshape(27, 32, 64)
    w3 = jnp.transpose(w_third, (2, 3, 4, 0, 1)).reshape(27, 64, 64)
    anywhere = pl.BlockSpec(memory_space=pltpu.HBM)
    dma = pltpu.SemaphoreType.DMA
    return pl.pallas_call(
        functools.partial(kernel, nx, ny),
        out_shape=jax.ShapeDtypeStruct((64, 2, 8, 128), BF),
        in_specs=[anywhere] * 7,
        out_specs=pl.BlockSpec(memory_space=pltpu.VMEM),
        scratch_shapes=[
            pltpu.VMEM((6, 32, 16, 256), BF),
            pltpu.VMEM((27, 32, 32), BF),
            pltpu.VMEM((27, 32, 64), BF),
            pltpu.VMEM((27, 64, 64), BF),
            pltpu.VMEM((27, 32, 512), F32),
            pltpu.VMEM((27, 64, 256), F32),
            pltpu.VMEM((27, 64, 512), F32),
            pltpu.VMEM((512, 4608), BF),
            pltpu.VMEM((512, 2304), BF),
            pltpu.VMEM((512, 4608), BF),
            pltpu.VMEM((9216, 256), BF),
            pltpu.VMEM((4, 512, 256), F32),
            pltpu.VMEM((256, 512), BF),
            pltpu.VMEM((128, 256), BF),
            pltpu.VMEM((6, 8, 512), BF),
            pltpu.VMEM((8, 512), BF),
            pltpu.VMEM((72, 2688), BF),
            pltpu.VMEM((2, 256, 128), BF),
            pltpu.VMEM((2, 256, 128), BF),
            pltpu.VMEM((2, 256, 128), BF),
            pltpu.VMEM((9, 8, 256), BF),
            pltpu.VMEM((8, 256), BF),
            pltpu.VMEM((768, 256), BF),
            pltpu.VMEM((768, 256), BF),
            pltpu.VMEM((768, 256), BF),
            pltpu.VMEM((768, 256), BF),
            pltpu.VMEM((2304, 128), BF),
            pltpu.VMEM((512, 512), F32),
            pltpu.VMEM((512, 640), BF),
            pltpu.VMEM((4608, 256), BF),
            pltpu.VMEM((256, 128), F32),
            pltpu.VMEM((512, 128), F32),
            pltpu.VMEM((512, 128), F32),
            pltpu.SMEM((32,), F32),
            pltpu.SMEM((64,), F32),
            pltpu.SMEM((64,), F32),
            dma((10,)), dma((2, 2)), dma((2, 2)), dma((6,)), dma((6,)),
            dma((2, 2)), dma((2, 2)), dma((8,)), dma((8,)),
        ],
        compiler_params=pltpu.CompilerParams(
            collective_id=0, has_side_effects=True, vmem_limit_bytes=48 * 1024 * 1024),
        name="encoder",
    )(*(pltpu.with_memory_space_constraint(v, pltpu.HBM)
        for v in (image, w1, b_first, w2, b_second, w3, b_third)))


def solution(mesh):
    placed = (P(None, "gx", None, "gy"), P(), P(), P(), P(), P(), P())
    return jax.shard_map(
        per_device, mesh=mesh, in_specs=placed, out_specs=P(None, "gx", None, "gy"), check_vma=False
    )
```
